32 devices in a mesh: dp: 8 (over z, x), row: 2 (over y), col: 2 (over core).
Axes of the slice: x: 2, y: 2, z: 4, core: 2. Of those that a mesh axis runs over, the one named last changes fastest.
Arguments:
- hidden_in: bfloat16 [2048, 768], P('dp', ('row', 'col')), may hold values from -6 to 6
- encoder_states: bfloat16 [4096, 768], P('dp', ('row', 'col')), may hold values from -6 to 6
- token_segments: int32 [8, 256], P('dp'), may hold values from 0 to 2, never falling along the last dimension, each value on 1 to 152 neighbouring positions
- source_segments: int32 [8, 512], P('dp'), may hold values from 0 to 2, never falling along the last dimension, each value on 1 to 304 neighbouring positions
- buckets: int32 [256, 256], replicated, may hold values from 0 to 31
- gain_self: float32 [768], P(('row', 'col')), may hold values from 0.5 to 1.5
- gain_cross: float32 [768], P(('row', 'col')), may hold values from 0.5 to 1.5
- gain_feed: float32 [768], P(('row', 'col')), may hold values from 0.5 to 1.5
- self_querykey: bfloat16 [768, 1536], P('row', 'col'), may hold values from -0.078125 to 0.078125
- self_value: bfloat16 [768, 768], P('row', 'col'), may hold values from -0.21875 to 0.21875
- self_output: bfloat16 [768, 768], P('col', 'row'), may hold values from -0.875 to 0.875
- cross_query: bfloat16 [768, 768], P('row', 'col'), may hold values from -0.0546875 to 0.0546875
- cross_keyvalue: bfloat16 [768, 1536], P('row', 'col'), may hold values from -0.15625 to 0.15625
- cross_output: bfloat16 [768, 768], P('col', 'row'), may hold values from -0.875 to 0.875
- gate_weight: bfloat16 [768, 2048], P('row', 'col'), may hold values from -0.21875 to 0.21875
- up_weight: bfloat16 [768, 2048], P('row', 'col'), may hold values from -0.21875 to 0.21875
- down_weight: bfloat16 [2048, 768], P('col', 'row'), may hold values from -0.125 to 0.125
- bias_table: float32 [32, 12], P(None, ('col', 'row')), may hold values from -6 to 6
- cotangent: bfloat16 [2048, 768], P('dp', ('row', 'col')), may hold values from -6 to 6
Outputs:
- hidden_out: bfloat16 [2048, 768], P('dp', ('row', 'col'))
- grad_hidden: float32 [2048, 768], P('dp', ('row', 'col'))
- grad_encoder: float32 [4096, 768], P('dp', ('row', 'col'))
- querykey_grad: float32 [768, 1536], P(('row', 'dp'), 'col')
- value_grad: float32 [768, 768], P(('row', 'dp'), 'col')
- output_grad: float32 [768, 768], P(('col', 'dp'), 'row')
- crossquery_grad: float32 [768, 768], P(('row', 'dp'), 'col')
- keyvalue_grad: float32 [768, 1536], P(('row', 'dp'), 'col')
- crossout_grad: float32 [768, 768], P(('col', 'dp'), 'row')
- gate_grad: float32 [768, 2048], P(('row', 'dp'), 'col')
- upweight_grad: float32 [768, 2048], P(('row', 'dp'), 'col')
- down_grad: float32 [2048, 768], P(('col', 'dp'), 'row')
- gainself_grad: float32 [768], P(('row', 'col'))
- gaincross_grad: float32 [768], P(('row', 'col'))
- gainfeed_grad: float32 [768], P(('row', 'col'))
- table_grad: float32 [32, 12], P(None, ('col', 'row'))
The draws below stay inside these ranges and needn't reach their ends.
Inputs may be any that keep to these rules, and one draw needn't show every extreme that they name: `token_segments`: in each sequence the numbers never fall, every value from 0 to 2 occurs, and no document has more than 152 tokens. `source_segments`: in each sequence the numbers never fall, every value from 0 to 2 occurs, and no document has more than 304 positions.
All inputs are finite; a program needn't handle non-finite values.
Results may differ from the reference program's by a relative error of at most 0.02.
Values may be sent and summed in bfloat16 or wider, within the bound.
No kernel may reach another device: no remote copies, remote signals or barrier semaphores. Data moves between devices by JAX's collectives and lax.ppermute only.
A program may use at most 128 MiB of HBM per device.

```python
import math
import jax
import jax.numpy as jnp
import numpy as np
from jax import lax

D = 768
H = 12
DH = 64
FF = 2048
NB = 32
SEQ = 256
ELEN = 512
DOCS = 3
HD = 768
NSEQ = 8
TOKENS = 2048
SOURCES = 4096
DOC_MOST = 152
SRC_MOST = 304


def place_ends(values, key, low, high):
    index_at = [jax.random.randint(jax.random.fold_in(key, axis), (), 0, length) for axis, length in enumerate(values.shape)]
    longest = values.shape.index(max(values.shape))
    neighbour = index_at[:longest] + [(index_at[longest] + 1) % values.shape[longest]] + index_at[longest + 1:]
    return values.at[tuple(index_at)].set(low).at[tuple(neighbour)].set(high)


def with_spikes(values, stream_key, source, target, blocks, factor):
    owner, partner = [(jnp.arange(values.shape[axis_at]) // (values.shape[axis_at] // blocks)).reshape([-1 if axis == axis_at else 1 for axis in range(values.ndim)]) for axis_at in (source, target)]
    chosen = jax.random.permutation(stream_key, blocks)[partner]
    strong = (owner == chosen) | (owner == (partner + blocks // 2) % blocks)
    return jnp.where(strong, factor * values, values)


def block_levels(key, extent, cuts, least, largest):
    loudness = 1.0
    for dim, shards_of in cuts:
        draws = jax.random.uniform(jax.random.fold_in(jax.random.fold_in(key, 6), dim), (shards_of,), jnp.float32, least / len(cuts), largest / len(cuts))
        loudness = loudness * jnp.repeat(jnp.exp(draws), extent[dim] // shards_of).reshape((-1,) + (1,) * (len(extent) - 1 - dim))
    return loudness


def profile(count, total, reach, slope):
    loads = [(1 << 20) // math.isqrt(grade ** slope) + 1 for grade in range(2, count + 1)]
    rest, given = total - reach - (count - 1), [1] * (count - 1)
    while rest > 0:
        movable = [i for i in range(count - 1) if given[i] < reach]
        mass, left = sum([loads[i] for i in movable]), rest
        for i in movable:
            more = min(reach - given[i], max(1, left * loads[i] // mass), rest)
            given[i] = given[i] + more
            rest = rest - more
    return np.array([reach] + given)


def ragged(rng, amount, total, most, slope):
    if amount == 2:
        one = jax.random.randint(rng, (), max(1, total - most), min(most, total - 1) + 1)
        return jnp.stack([one, total - one])
    sizes = jnp.asarray(profile(amount, total, most, slope), jnp.int32)
    pairs = (amount - 1) // 2
    giver, receiver = sizes[1:1 + 2 * pairs:2], sizes[2:2 + 2 * pairs:2]
    room = jnp.minimum(giver - 1, most - receiver)
    moved = jax.random.randint(jax.random.fold_in(rng, 1), (pairs,), 0, 1 << 20) % (room + 1)
    sizes = sizes.at[1:1 + 2 * pairs:2].set(giver - moved).at[2:2 + 2 * pairs:2].set(receiver + moved)
    return sizes[jax.random.permutation(jax.random.fold_in(rng, 2), amount)]


def scatter_about(rng, extent, scale, most, cuts=(), kind=jnp.bfloat16):
    drawn = scale * jax.random.normal(rng, extent, jnp.float32)
    if cuts:
        drawn = drawn * block_levels(rng, extent, cuts, -0.22, 0.18)
    return jnp.clip(drawn, -most, most).astype(kind)


def gaussian_with(own_key, extent, deviation, reach, cuts, heavy, kind=jnp.bfloat16):
    values = deviation * jax.random.normal(own_key, extent, jnp.float32)
    if cuts:
        values = values * block_levels(own_key, extent, cuts, -0.22, 0.18)
    return jnp.clip(with_spikes(values, jax.random.fold_in(own_key, 3), *heavy), -reach, reach).astype(kind)


def setup_inputs(seed: int = 0) -> dict:
    arg_keys = jax.random.split(jax.random.key(seed), 20)
    return {
        "hidden_in": gaussian_with(arg_keys[0], (TOKENS, D), 1.0, 6.0, ((0, 8), (1, 4)), (0, 1, 8, 2.0)),
        "encoder_states": scatter_about(arg_keys[1], (SOURCES, D), 1.0, 6.0, ((0, 8), (1, 4))),
        "token_segments": jax.vmap(lambda own: jnp.searchsorted(jnp.cumsum(ragged(own, DOCS, SEQ, DOC_MOST, 0)), jnp.arange(SEQ), side="right"))(jax.random.split(arg_keys[2], NSEQ)).reshape((NSEQ, SEQ)).astype(jnp.int32),
        "source_segments": jax.vmap(lambda own: jnp.searchsorted(jnp.cumsum(ragged(own, DOCS, ELEN, SRC_MOST, 0)), jnp.arange(ELEN), side="right"))(jax.random.split(arg_keys[3], NSEQ)).reshape((NSEQ, ELEN)).astype(jnp.int32),
        "buckets": place_ends(jax.random.randint(arg_keys[4], (SEQ, SEQ), 0, NB), jax.random.fold_in(arg_keys[4], 1), 0, NB - 1).astype(jnp.int32),
        "gain_self": jnp.clip(1.0 + 0.1 * jax.random.normal(arg_keys[5], (D,), jnp.float32), 0.5, 1.5),
        "gain_cross": jnp.clip(1.0 + 0.1 * jax.random.normal(arg_keys[6], (D,), jnp.float32), 0.5, 1.5),
        "gain_feed": jnp.clip(1.0 + 0.1 * jax.random.normal(arg_keys[7], (D,), jnp.float32), 0.5, 1.5),
        "self_querykey": scatter_about(arg_keys[8], (D, 2 * HD), (8 * D) ** -0.5, 0.078125, ((0, 2), (1, 2))),
        "self_value": scatter_about(arg_keys[9], (D, HD), D ** -0.5, 0.21875, ((0, 2), (1, 2))),
        "self_output": scatter_about(arg_keys[10], (HD, D), (HD // 16) ** -0.5, 0.875, ((0, 2), (1, 2))),
        "cross_query": scatter_about(arg_keys[11], (D, HD), (16 * D) ** -0.5, 0.0546875, ((0, 2), (1, 2))),
        "cross_keyvalue": scatter_about(arg_keys[12], (D, 2 * HD), (2 * D) ** -0.5, 0.15625, ((0, 2), (1, 2))),
        "cross_output": scatter_about(arg_keys[13], (HD, D), (HD // 16) ** -0.5, 0.875, ((0, 2), (1, 2))),
        "gate_weight": scatter_about(arg_keys[14], (D, FF), D ** -0.5, 0.21875, ((0, 2), (1, 2))),
        "up_weight": scatter_about(arg_keys[15], (D, FF), D ** -0.5, 0.21875, ((0, 2), (1, 2))),
        "down_weight": scatter_about(arg_keys[16], (FF, D), FF ** -0.5, 0.125, ((0, 2), (1, 2))),
        "bias_table": scatter_about(arg_keys[17], (NB, H), 1.0, 6.0, ((1, 4),), jnp.float32),
        "cotangent": gaussian_with(arg_keys[18], (TOKENS, D), 1.0, 6.0, ((0, 8), (1, 4)), (0, 1, 8, 2.0)),
    }


EPS = 1e-06
ROOT = 0.7978845608028654
CUBIC = 0.044715

def gelu_tanh(value):
    return 0.5 * value * (1.0 + jnp.tanh(ROOT * (value + CUBIC * value * value * value)))

def gelu_slope(value):
    inner = jnp.tanh(ROOT * (value + CUBIC * value * value * value))
    return 0.5 * (1.0 + inner) + 0.5 * value * (1.0 - inner * inner) * ROOT * (1.0 + 3.0 * CUBIC * value * value)

def matmul(left, right):
    return jnp.dot(left, right, preferred_element_type=jnp.float32)

def widen(values):
    return lax.optimization_barrier(values).astype(jnp.float32)

def rms_norm(resid, gain):
    scale = lax.rsqrt(lax.optimization_barrier(jnp.mean(resid * resid, axis=1)) + EPS)
    return ((resid * scale[:, None] * gain).astype(jnp.bfloat16), scale)

def rms_back(upstream, resid, scale, gain):
    normed = resid * scale[:, None]
    scaled = upstream * gain
    grad = scale[:, None] * (scaled - normed * lax.optimization_barrier(jnp.mean(scaled * normed, axis=1))[:, None])
    return (grad, lax.optimization_barrier(jnp.sum(upstream * normed, axis=0)))

def masked_scores(queries, keys, bias, allowed):
    scores = jnp.einsum('qhd,khd->hqk', widen(queries), widen(keys)) + bias
    return jnp.where(allowed[None], scores, -jnp.inf)

def attend(scores, values):
    top = lax.optimization_barrier(jnp.max(scores, axis=2, keepdims=True))
    logsum = top[:, :, 0] + jnp.log(lax.optimization_barrier(jnp.sum(jnp.exp(scores - top), axis=2)))
    probs = jnp.exp(scores - logsum[:, :, None]).astype(jnp.bfloat16)
    mixed = jnp.einsum('hqk,khd->qhd', widen(probs), widen(values))
    return (mixed.astype(jnp.bfloat16), logsum)

def attend_back(scores, logsum, queries, keys, values, mixed, upstream):
    probs = jnp.exp(scores - logsum[:, :, None])
    drift = jnp.einsum('qhd,khd->hqk', widen(upstream), widen(values))
    centre = lax.optimization_barrier(jnp.sum(widen(upstream) * widen(mixed), axis=2))
    dscores = probs * (drift - jnp.transpose(centre)[:, :, None])
    lowered = widen(dscores.astype(jnp.bfloat16))
    grad_query = jnp.einsum('hqk,khd->qhd', lowered, widen(keys)).astype(jnp.bfloat16)
    grad_key = jnp.einsum('hqk,qhd->khd', lowered, widen(queries)).astype(jnp.bfloat16)
    grad_value = jnp.einsum('hqk,qhd->khd', widen(probs.astype(jnp.bfloat16)), widen(upstream)).astype(jnp.bfloat16)
    return (grad_query, grad_key, grad_value, dscores)

def reference(hidden_in, encoder_states, token_segments, source_segments, buckets, gain_self, gain_cross, gain_feed, self_querykey, self_value, self_output, cross_query, cross_keyvalue, cross_output, gate_weight, up_weight, down_weight, bias_table, cotangent):
    position_bias = jnp.transpose(bias_table[buckets], (2, 0, 1))
    places = jnp.arange(SEQ, dtype=jnp.int32)
    causal = places[None, :] <= places[:, None]
    shapes = [self_querykey, self_value, self_output, cross_query, cross_keyvalue, cross_output, gate_weight, up_weight, down_weight, gain_self, gain_cross, gain_feed]
    start_sums = tuple([jnp.zeros(array.shape, jnp.float32) for array in shapes])
    start_grid = jnp.zeros((H, SEQ, SEQ), jnp.float32)

    def one_sequence(carry, pieces):
        sums, grid = carry
        inputs, source_states, segment, source, upstream_out = pieces
        resid_in = inputs.astype(jnp.float32)
        normed_self, scale_self = rms_norm(resid_in, gain_self)
        query_key = matmul(normed_self, self_querykey).astype(jnp.bfloat16).reshape(SEQ, H, 2, DH)
        value_rows = matmul(normed_self, self_value).astype(jnp.bfloat16).reshape(SEQ, H, DH)
        allowed_self = causal & (segment[:, None] == segment[None, :])
        scores_self = masked_scores(query_key[:, :, 0], query_key[:, :, 1], position_bias, allowed_self)
        self_mixed, self_lse = attend(scores_self, value_rows)
        self_flat = self_mixed.reshape(SEQ, HD)
        resid_attn = resid_in + matmul(self_flat, self_output)
        normed_cross, scale_cross = rms_norm(resid_attn, gain_cross)
        cross_q = matmul(normed_cross, cross_query).astype(jnp.bfloat16).reshape(SEQ, H, DH)
        cross_kv = matmul(source_states, cross_keyvalue).astype(jnp.bfloat16).reshape(ELEN, H, 2, DH)
        allowed_cross = segment[:, None] == source[None, :]
        scores_cross = masked_scores(cross_q, cross_kv[:, :, 0], 0.0, allowed_cross)
        cross_mixed, cross_lse = attend(scores_cross, cross_kv[:, :, 1])
        cross_flat = cross_mixed.reshape(SEQ, HD)
        resid_cross = resid_attn + matmul(cross_flat, cross_output)
        normed_feed, scale_feed = rms_norm(resid_cross, gain_feed)
        gate_act = matmul(normed_feed, gate_weight)
        up_act = matmul(normed_feed, up_weight)
        gelu_gate = gelu_tanh(gate_act)
        feed_hidden = (gelu_gate * up_act).astype(jnp.bfloat16)
        hidden_out = (resid_cross + matmul(feed_hidden, down_weight)).astype(jnp.bfloat16)
        down_term = matmul(feed_hidden.T, upstream_out)
        grad_feed = matmul(upstream_out, down_weight.T)
        gate_delta = (grad_feed * up_act * gelu_slope(gate_act)).astype(jnp.bfloat16)
        up_delta = (grad_feed * gelu_gate).astype(jnp.bfloat16)
        gate_term = matmul(normed_feed.T, gate_delta)
        up_term = matmul(normed_feed.T, up_delta)
        grad_normed_feed = matmul(gate_delta, gate_weight.T) + matmul(up_delta, up_weight.T)
        back_feed, feed_gain_term = rms_back(grad_normed_feed, resid_cross, scale_feed, gain_feed)
        grad_resid_cross = upstream_out.astype(jnp.float32) + back_feed
        cross_upstream = grad_resid_cross.astype(jnp.bfloat16)
        crossout_term = matmul(cross_flat.T, cross_upstream)
        cross_delta = matmul(cross_upstream, cross_output.T).astype(jnp.bfloat16).reshape(SEQ, H, DH)
        cross_dq, cross_dkey, cross_dvalue, unused = attend_back(scores_cross, cross_lse, cross_q, cross_kv[:, :, 0], cross_kv[:, :, 1], cross_mixed, cross_delta)
        cross_dq = cross_dq.reshape(SEQ, HD)
        cross_dkv = jnp.stack((cross_dkey, cross_dvalue), axis=2).reshape(ELEN, 2 * HD)
        crossquery_term = matmul(normed_cross.T, cross_dq)
        keyvalue_term = matmul(source_states.T, cross_dkv)
        grad_source = matmul(cross_dkv, cross_keyvalue.T)
        grad_normed_cross = matmul(cross_dq, cross_query.T)
        back_cross, cross_gain_term = rms_back(grad_normed_cross, resid_attn, scale_cross, gain_cross)
        grad_resid_attn = grad_resid_cross + back_cross
        self_upstream = grad_resid_attn.astype(jnp.bfloat16)
        output_term = matmul(self_flat.T, self_upstream)
        self_delta = matmul(self_upstream, self_output.T).astype(jnp.bfloat16).reshape(SEQ, H, DH)
        self_dquery, self_dkey, self_dvalue, self_dscores = attend_back(scores_self, self_lse, query_key[:, :, 0], query_key[:, :, 1], value_rows, self_mixed, self_delta)
        grad_query_key = jnp.stack((self_dquery, self_dkey), axis=2).reshape(SEQ, 2 * HD)
        grad_value_rows = self_dvalue.reshape(SEQ, HD)
        querykey_term = matmul(normed_self.T, grad_query_key)
        value_term = matmul(normed_self.T, grad_value_rows)
        grad_normed_self = matmul(grad_query_key, self_querykey.T) + matmul(grad_value_rows, self_value.T)
        back_self, self_gain_term = rms_back(grad_normed_self, resid_in, scale_self, gain_self)
        grad_input = grad_resid_attn + back_self
        terms = (querykey_term, value_term, output_term, crossquery_term, keyvalue_term, crossout_term, gate_term, up_term, down_term, self_gain_term, cross_gain_term, feed_gain_term)
        sums = tuple([total + term for total, term in zip(sums, terms)])
        return ((sums, grid + self_dscores), (hidden_out, grad_input, grad_source))
    pieces = (hidden_in.reshape(NSEQ, SEQ, D), encoder_states.reshape(NSEQ, ELEN, D), token_segments, source_segments, cotangent.reshape(NSEQ, SEQ, D))
    (sums, grid), (outputs, grad_inputs, grad_sources) = lax.scan(one_sequence, (start_sums, start_grid), pieces)
    table_grad = jax.ops.segment_sum(jnp.transpose(grid.reshape(H, SEQ * SEQ)), buckets.reshape(-1).astype(jnp.int32), num_segments=NB)
    return (outputs.reshape(TOKENS, D), grad_inputs.reshape(TOKENS, D), grad_sources.reshape(SOURCES, D), sums[0], sums[1], sums[2], sums[3], sums[4], sums[5], sums[6], sums[7], sums[8], sums[9], sums[10], sums[11], table_grad)
```

```python
import jax
import jax.numpy as jnp
from jax import lax
from jax.experimental import pallas as pl
from jax.experimental.pallas import tpu as pltpu
from jax.sharding import PartitionSpec as P


BF = jnp.bfloat16
F32 = jnp.float32
EPS = 1e-06
ROOT = 0.7978845608028654
CUBIC = 0.044715
MASKED = -1e30
SWAP = [(0, 1), (1, 0)]


def nn(left, right):
    return jnp.dot(left, right, preferred_element_type=F32)


def nt(left, right):
    return lax.dot_general(left, right, (((1,), (1,)), ((), ())), preferred_element_type=F32)


def tn(left, right):
    return lax.dot_general(left, right, (((0,), (0,)), ((), ())), preferred_element_type=F32)


def call(kernel, outs, *args):
    flat = [jax.ShapeDtypeStruct(shape, dtype) for shape, dtype in outs]
    space = pl.BlockSpec(memory_space=pltpu.VMEM)
    return pl.pallas_call(
        kernel,
        out_shape=flat,
        in_specs=[space] * len(args),
        out_specs=[space] * len(flat),
        compiler_params=pltpu.CompilerParams(vmem_limit_bytes=60 * 1024 * 1024),
    )(*args)


def row_swap(values):
    return lax.ppermute(values, "row", SWAP)


def col_swap(values):
    return lax.ppermute(values, "col", SWAP)


def own_rows(ref, base=0):
    half = 128
    start = base + lax.axis_index("col") * half
    return ref[pl.ds(pl.multiple_of(start, 16), half), :]


def each_side(axis, body):
    index = lax.axis_index(axis)
    for side in (0, 1):
        pl.when(index == side)(lambda side=side: body(side))


def swapped(ref, left, right):
    width = left.shape[1]
    ref[:, :width] = right.astype(BF)
    ref[:, width:] = left.astype(BF)


def each_replica(body):
    for part in range(4):
        pl.when(lax.axis_index("dp") % 4 == part)(lambda part=part: body(part))


def weight_parts(keep_body, send_body):
    def of_row(side):
        keep_body(side)
        each_replica(lambda part: send_body(1 - side, part))

    each_side("row", of_row)


def keep_cols(src, keep, at, width, side):
    keep[:, at : at + width] = src[:, side * width : (side + 1) * width]


def send_cols(src, send, at, width, side, part):
    rows = src.shape[0] // 4
    send[:, at : at + width] = src[
        part * rows : (part + 1) * rows, side * width : (side + 1) * width
    ]


def keep_out(src, keep, at, side):
    rows = src.shape[0] // 2
    width = src.shape[1] // 2
    for block in (0, 1):
        keep[block * rows : (block + 1) * rows, at : at + width] = src[
            side * rows : (side + 1) * rows, block * width : (block + 1) * width
        ]


def send_out(src, send, at, side, part):
    rows = src.shape[0] // 4
    width = src.shape[1] // 2
    start = side * 2 * rows + part % 2 * rows
    send[:, at : at + width] = src[
        start : start + rows, part // 2 * width : (part // 2 + 1) * width
    ]


def join_parts(parts, out):
    rows = parts[0].shape[0]
    place = lax.axis_index("dp") % 4
    for away, part in enumerate(parts):
        start = jnp.bitwise_xor(place, away) * rows
        out[pl.ds(pl.multiple_of(start, 16), rows), :] = part[...]


def assemble(own, recv, own_peer, recv_peer):
    core = lax.axis_index("col")
    first = core == 0
    quarters = (
        jnp.where(first, own[...], own_peer[...]),
        jnp.where(first, own_peer[...], own[...]),
        jnp.where(first, recv[...], recv_peer[...]),
        jnp.where(first, recv_peer[...], recv[...]),
    )
    return jnp.concatenate(quarters, axis=0)


def pack_three(wide, narrow, out, keep, send):
    def keep_body(side):
        keep_cols(wide, keep, 0, 384, side)
        keep_cols(narrow, keep, 384, 192, side)
        keep_out(out, keep, 576, side)

    def send_body(side, part):
        send_cols(wide, send, 0, 384, side, part)
        send_cols(narrow, send, 384, 192, side, part)
        send_out(out, send, 576, side, part)

    weight_parts(keep_body, send_body)


def prep_self(hidden, gs, gc, gf, qk, v, wo, packed, keep, send):
    tokens = hidden.shape[1]
    packed[:, :tokens] = hidden[...]
    gains = jnp.concatenate([gs[...], gc[...], gf[...]], axis=0)
    high = gains.astype(BF)
    low = (gains - high.astype(F32)).astype(BF)
    rows = jnp.concatenate(
        [high.astype(F32), low.astype(F32), jnp.zeros((10, gains.shape[1]), F32)], axis=0
    ).astype(BF)
    line = lax.broadcasted_iota(jnp.int32, (16, 16), 0)
    place = lax.broadcasted_iota(jnp.int32, (16, 16), 1)
    packed[:, tokens:] = tn(rows, jnp.where(line == place, 1.0, 0.0).astype(BF)).astype(BF)

    pack_three(qk, v, wo, keep, send)


def prep_cross(enc, cot, q, kv, wo, packed, keep, send):
    packed[:, : enc.shape[1]] = enc[...]
    packed[:, enc.shape[1] :] = cot[...]

    pack_three(kv, q, wo, keep, send)


def prep_feed(gate, up, down, keep, send, keep_down, send_down):
    def keep_body(side):
        keep_cols(gate, keep, 0, 512, side)
        keep_cols(up, keep, 512, 512, side)
        keep_down[...] = down[side * 512 : (side + 1) * 512, :]

    def send_body(side, part):
        send_cols(gate, send, 0, 512, side, part)
        send_cols(up, send, 512, 512, side, part)
        at = side * 512 + part * 128
        send_down[...] = down[at : at + 128, :]

    weight_parts(keep_body, send_body)


def masks(buckets, table, peer_table, segment, source, bias_out, cross_out):
    core = lax.axis_index("col")
    ids = own_rows(buckets)
    rows, cols = ids.shape
    line = lax.broadcasted_iota(jnp.int32, (rows, cols), 0) + core * rows
    place = lax.broadcasted_iota(jnp.int32, (rows, cols), 1)
    keys = segment[...]
    mine = jnp.sum(
        jnp.where(place == line, jnp.broadcast_to(keys, (rows, cols)).astype(F32), 0.0),
        axis=1,
        keepdims=True,
    )
    allowed = (place <= line) & (keys.astype(F32) == mine)
    for head in range(6):
        ref = table if head < 3 else peer_table
        entries = jnp.broadcast_to(ref[head % 3 : head % 3 + 1, :], (rows, 128))
        parts = [
            jnp.take_along_axis(
                entries, ids[:, at : at + 128], axis=1, mode="promise_in_bounds"
            )
            for at in range(0, cols, 128)
        ]
        bias_out[head] = jnp.where(allowed, jnp.concatenate(parts, axis=1), MASKED)
    cross_out[...] = jnp.where(source[...].astype(F32) == mine, 0.0, MASKED)


def gain_row(gains, which):
    return gains[which : which + 1, :]


def norm(resid, gain):
    scale = lax.rsqrt(jnp.mean(resid * resid, axis=1, keepdims=True) + EPS)
    return resid * scale * gain, scale


def norm_back(upstream, resid, gain):
    scale = lax.rsqrt(jnp.mean(resid * resid, axis=1, keepdims=True) + EPS)
    normed = resid * scale
    scaled = upstream * gain
    grad = scale * (scaled - normed * jnp.mean(scaled * normed, axis=1, keepdims=True))
    return grad, jnp.sum(upstream * normed, axis=0, keepdims=True)


def project(left, top, bottom, at, width):
    return nn(left[:, :384], top[:, at : at + width]) + nn(left[:, 384:], bottom[:, at : at + width])


def softmax(scores):
    top = jnp.max(scores, axis=1, keepdims=True)
    weights = jnp.exp(scores - top)
    total = jnp.sum(weights, axis=1, keepdims=True)
    return (weights * (1.0 / total)).astype(BF), top + jnp.log(total)


def out_project(mixed, a0, a1, b0, b1, keep, send):
    first, second = mixed[:, :192], mixed[:, 192:]
    parts = []
    for a, b in ((a0, b0), (a1, b1)):
        for block in (0, 1):
            lines = slice(block * 192, (block + 1) * 192)
            parts.append(nn(first, a[lines, 576:]) + nn(second, b[lines, 576:]))
    mine = jnp.concatenate(parts[:2], axis=1)
    theirs = jnp.concatenate(parts[2:], axis=1)
    keep[:, :384] = mine
    keep[:, 384:] = theirs
    swapped(send, mine, theirs)


def out_back(upstream, w0, w1):
    total = None
    for half, w in ((0, w0), (1, w1)):
        for block in (0, 1):
            at = half * 384 + block * 192
            term = nt(upstream[:, at : at + 192], w[block * 192 : (block + 1) * 192, 576:])
            total = term if total is None else total + term
    return total


def self_forward(
    own, recv, own_peer, recv_peer, a0, b0, p0, p1, p2, p3, q0, q1, q2, q3, bias, x_out, gains_out, a1, b1, normed_out, ya, yb, mixed_out, lse_out, keep, send,
):
    join_parts((p0, p1, p2, p3), a1)
    join_parts((q0, q1, q2, q3), b1)
    tokens = normed_out.shape[0]
    whole = assemble(own, recv, own_peer, recv_peer).astype(F32)
    resid = jnp.transpose(whole[:, :tokens])
    x_out[...] = resid.astype(BF)
    parts = whole[:, tokens:].astype(BF)
    line = lax.broadcasted_iota(jnp.int32, (16, 16), 0)
    place = lax.broadcasted_iota(jnp.int32, (16, 16), 1)
    chosen = (line == place) | ((line == place - 3) & (place < 6))
    chosen = jnp.where(chosen & (line < 3), 1.0, 0.0).astype(BF)
    gains_out[...] = nt(chosen, parts)
    normed = norm(resid, gain_row(gains_out, 0))[0].astype(BF)
    normed_out[...] = normed
    ya[...] = project(normed, a0, a1, 0, 576).astype(BF)
    yb[...] = project(normed, b0, b1, 0, 576).astype(BF)
    mixed = []
    for head in range(6):
        y = ya if head < 3 else yb
        at = (head % 3) * 128
        mine = own_rows(y)
        scores = nt(mine[:, at : at + 64], y[:, at + 64 : at + 128]) + bias[head]
        probs, lse = softmax(scores)
        lse_out[head] = lse
        at = 384 + (head % 3) * 64
        mixed.append(nn(probs, y[:, at : at + 64]))
    mixed = jnp.concatenate(mixed, axis=1).astype(BF)
    mixed_out[...] = mixed
    out_project(mixed, a0, a1, b0, b1, keep, send)


def encode_keys(
    own, recv, own_peer, recv_peer, a0, b0, p0, p1, p2, p3, q0, q1, q2, q3, ec, a1, b1, kva, kvb,
):
    join_parts((p0, p1, p2, p3), a1)
    join_parts((q0, q1, q2, q3), b1)
    rows = kva.shape[0]
    whole = assemble(own, recv, own_peer, recv_peer).astype(F32)
    ec[...] = jnp.transpose(whole).astype(BF)
    enc = ec[:rows, :]
    kva[...] = project(enc, a0, a1, 0, 384).astype(BF)
    kvb[...] = project(enc, b0, b1, 0, 384).astype(BF)


def cross_forward(
    xg, gains, part, recv, a0, a1, b0, b1, kva, kvb, mask, resid_out, normed_out, q_out, mixed_out,
    lse_out, keep, send,
):
    resid = own_rows(xg).astype(F32) + part[...] + recv[...].astype(F32)
    resid_out[...] = resid
    normed = norm(resid, gain_row(gains, 1))[0].astype(BF)
    normed_out[...] = normed
    queries = jnp.concatenate(
        [project(normed, a0, a1, 384, 192), project(normed, b0, b1, 384, 192)], axis=1
    ).astype(BF)
    q_out[...] = queries
    mixed = []
    for head in range(6):
        kv = kva if head < 3 else kvb
        at = (head % 3) * 128
        scores = nt(queries[:, head * 64 : head * 64 + 64], kv[:, at : at + 64]) + mask[...]
        probs, lse = softmax(scores)
        lse_out[head] = lse
        mixed.append(nn(probs, kv[:, at + 64 : at + 128]))
    mixed = jnp.concatenate(mixed, axis=1).astype(BF)
    mixed_out[...] = mixed
    out_project(mixed, a0, a1, b0, b1, keep, send)


def feed_upstream(ec, da0, db0, *refs):
    parts, (fa1, fb1, da1, db1, out) = refs[:16], refs[16:]
    for at, ref in enumerate((fa1, fb1, da1, db1)):
        join_parts(parts[at * 4 : at * 4 + 4], ref)
    cot = own_rows(ec, ec.shape[0] - 256)
    out[:, :512] = nt(cot[:, :384], da0[...]) + nt(cot[:, 384:], da1[...])
    out[:, 512:] = nt(cot[:, :384], db0[...]) + nt(cot[:, 384:], db1[...])


def feed_forward(
    xg, gains, prior, part, recv, fa0, fa1, fb0, fb1, upstream, resid_out, normed_out, hidden_out,
    gate_out, up_out, keep, send,
):
    resid = prior[...] + part[...] + recv[...].astype(F32)
    resid_out[...] = resid
    normed = norm(resid, gain_row(gains, 2))[0].astype(BF)
    normed_out[...] = normed
    deltas = []
    for side, (w0, w1) in enumerate(((fa0, fa1), (fb0, fb1))):
        lanes = slice(side * 512, side * 512 + 512)
        gate = project(normed, w0, w1, 0, 512)
        up = project(normed, w0, w1, 512, 512)
        inner = jnp.tanh(ROOT * (gate + CUBIC * gate * gate * gate))
        gelu = 0.5 * gate * (1.0 + inner)
        slope = 0.5 * (1.0 + inner) + 0.5 * gate * (1.0 - inner * inner) * ROOT * (
            1.0 + 3.0 * CUBIC * gate * gate
        )
        grad = upstream[:, lanes]
        hidden_out[:, lanes] = (gelu * up).astype(BF)
        gate_delta = (grad * up * slope).astype(BF)
        up_delta = (grad * gelu).astype(BF)
        gate_out[:, lanes] = gate_delta
        up_out[:, lanes] = up_delta
        deltas.append((gate_delta, up_delta))
    (ga, ua), (gb, ub) = deltas
    mine = nt(ga, fa0[:, :512]) + nt(ua, fa0[:, 512:]) + nt(gb, fb0[:, :512]) + nt(ub, fb0[:, 512:])
    theirs = (
        nt(ga, fa1[:, :512]) + nt(ua, fa1[:, 512:]) + nt(gb, fb1[:, :512]) + nt(ub, fb1[:, 512:])
    )
    keep[:, :384] = mine
    keep[:, 384:] = theirs
    swapped(send, mine, theirs)


def feed_grads(normed, gate, up, in_keep, in_send):
    left = normed[...]
    for ref, lanes in ((in_send, slice(512, 1024)), (in_keep, slice(0, 512))):
        ref[:, :512] = tn(left, gate[:, lanes]).astype(BF)
        ref[:, 512:] = tn(left, up[:, lanes]).astype(BF)


def feed_out(hidden, ec, resid, da0, da1, db0, db1, out_keep, out_send, last_keep, last_send):
    cot = own_rows(ec, ec.shape[0] - 256)
    out_send[...] = tn(hidden[:, 512:], cot).astype(BF)
    out_keep[...] = tn(hidden[:, :512], cot).astype(BF)
    last_send[...] = (nn(hidden[:, :512], da1[...]) + nn(hidden[:, 512:], db1[...])).astype(BF)
    last_keep[...] = (
        nn(hidden[:, :512], da0[...]) + nn(hidden[:, 512:], db0[...]) + resid[:, :384]
    )


def last_out(part, recv, keep, send):
    total = jnp.transpose(part[...] + recv[...].astype(F32)).astype(BF)

    def body(side):
        keep[...] = total[side * 192 : side * 192 + 192, :]
        send[...] = total[(1 - side) * 192 : (2 - side) * 192, :]

    each_side("col", body)


def store_grads(ref, left, wide, narrow, narrow_left):
    ref[:768, :] = tn(left, wide).astype(BF)
    thin = tn(narrow_left, narrow).astype(BF)
    ref[768:, :192] = thin[:384, :]
    ref[768:, 192:] = thin[384:, :]


def cross_backward(
    xg, gains, ec, part, recv, resid_in, a0, a1, b0, b1, q, kva, kvb, lse, mask, mixed, resid_out,
    upstream_out, gain_out, delta_out, dscores_out, probs_out, dq_out, keep, send,
):
    back, gain = norm_back(part[...] + recv[...].astype(F32), resid_in[...], gain_row(gains, 2))
    gain_out[...] = jnp.broadcast_to(gain, gain_out.shape)
    resid = own_rows(ec, ec.shape[0] - 256).astype(F32) + back
    resid_out[...] = resid
    upstream = resid.astype(BF)
    upstream_out[...] = upstream
    delta = jnp.concatenate(
        [out_back(upstream, a0, a1), out_back(upstream, b0, b1)], axis=1
    ).astype(BF)
    delta_out[...] = delta
    grads = []
    for head in range(6):
        kv = kva if head < 3 else kvb
        at = (head % 3) * 128
        lanes = slice(head * 64, head * 64 + 64)
        scores = nt(q[:, lanes], kv[:, at : at + 64]) + mask[...]
        probs = jnp.exp(scores - lse[head])
        probs_out[head] = probs.astype(BF)
        drift = nt(delta[:, lanes], kv[:, at + 64 : at + 128])
        centre = jnp.sum(
            delta[:, lanes].astype(F32) * mixed[:, lanes].astype(F32), axis=1, keepdims=True
        )
        low = (probs * (drift - centre)).astype(BF)
        dscores_out[head] = low
        grads.append(nn(low, kv[:, at : at + 64]))
    grads = jnp.concatenate(grads, axis=1).astype(BF)
    dq_out[...] = grads
    first, second = grads[:, :192], grads[:, 192:]
    mine = nt(first, a0[:, 384:576]) + nt(second, b0[:, 384:576])
    theirs = nt(first, a1[:, 384:576]) + nt(second, b1[:, 384:576])
    keep[:, :384] = mine
    keep[:, 384:] = theirs
    swapped(send, mine, theirs)


def cross_grads(
    ec, normed, q, delta, dscores, probs, dq, mixed, upstream, a0, a1, b0, b1, in_keep, in_send,
    out_keep, out_send, enc_keep, enc_send,
):
    rows = ec.shape[0] - 256
    enc = ec[:rows, :]
    left = normed[...]
    both = []
    for first in (0, 3):
        parts = []
        for head in range(first, first + 3):
            lanes = slice(head * 64, head * 64 + 64)
            parts.append(tn(dscores[head], q[:, lanes]))
            parts.append(tn(probs[head], delta[:, lanes]))
        both.append(jnp.concatenate(parts, axis=1).astype(BF))
    for ref, side in ((in_send, 1), (in_keep, 0)):
        store_grads(ref, enc, both[side], dq[:, side * 192 : side * 192 + 192], left)
    out_send[...] = tn(mixed[:, 192:], upstream[...]).astype(BF)
    out_keep[...] = tn(mixed[:, :192], upstream[...]).astype(BF)
    for half, (a, b) in enumerate(((a0, b0), (a1, b1))):
        total = nt(a[:, :384], both[0]) + nt(b[:, :384], both[1])

        def body(side, half=half, total=total):
            enc_keep[half] = total[side * 192 : side * 192 + 192, :]
            enc_send[half] = total[(1 - side) * 192 : (2 - side) * 192, :].astype(BF)

        each_side("col", body)


def self_backward(
    xg, gains, part, recv, upper, resid_in, a0, a1, b0, b1, normed, ya, yb, bias, lse, mixed, resid_out,
    gain_out, dscores_out, dya, dyb, in_keep, in_send, out_keep, out_send,
):
    back, gain = norm_back(part[...] + recv[...].astype(F32), resid_in[...], gain_row(gains, 1))
    gain_out[...] = jnp.broadcast_to(gain, gain_out.shape)
    resid = upper[...] + back
    resid_out[...] = resid
    upstream = resid.astype(BF)
    delta = jnp.concatenate(
        [out_back(upstream, a0, a1), out_back(upstream, b0, b1)], axis=1
    ).astype(BF)
    out_send[...] = tn(mixed[:, 192:], upstream).astype(BF)
    out_keep[...] = tn(mixed[:, :192], upstream).astype(BF)
    core = lax.axis_index("col").astype(F32)
    for y, dy, first in ((yb, dyb, 3), (ya, dya, 0)):
        mine = own_rows(y)
        pairs, values = [], []
        for head in range(first, first + 3):
            at = (head % 3) * 128
            vat = 384 + (head % 3) * 64
            lanes = slice(head * 64, head * 64 + 64)
            queries = mine[:, at : at + 64]
            scores = nt(queries, y[:, at + 64 : at + 128]) + bias[head]
            probs = jnp.exp(scores - lse[head])
            up = delta[:, lanes]
            drift = nt(up, y[:, vat : vat + 64])
            centre = jnp.sum(
                up.astype(F32) * mixed[:, lanes].astype(F32), axis=1, keepdims=True
            )
            dscores = probs * (drift - centre)
            dscores_out[head] = dscores
            low = dscores.astype(BF)
            dq = nn(low, y[:, at + 64 : at + 128])
            dq = jnp.concatenate([dq * (1.0 - core), dq * core], axis=0)
            pairs.append(jnp.concatenate([dq, tn(low, queries)], axis=1))
            values.append(tn(probs.astype(BF), up))
        dy[...] = jnp.concatenate(pairs + values, axis=1).astype(BF)
    left = normed[...]
    for ref, dy in ((in_send, dyb), (in_keep, dya)):
        store_grads(ref, left, dy[:, :384], dy[:, 384:], left)


def self_inputs(dya, dyb, a0, a1, b0, b1, keep, send):
    da, db = dya[...], dyb[...]
    totals = [nt(da, a[:, :576]) + nt(db, b[:, :576]) for a, b in ((a0, b0), (a1, b1))]

    def body(side):
        mine = slice(side * 128, side * 128 + 128)
        theirs = slice((1 - side) * 128, (1 - side) * 128 + 128)
        for at, total in ((0, totals[0]), (384, totals[1])):
            keep[:, at : at + 384] = total[mine, :]
            send[:, at : at + 384] = total[theirs, :].astype(BF)

    each_side("col", body)


def self_sum(part, other, keep, send):
    total = part[...] + other[...].astype(F32)
    keep[...] = total
    swapped(send, total[:, :384], total[:, 384:])


def table_sums(buckets, dscores, out):
    ids = own_rows(buckets)
    totals = []
    for head in range(6):
        grid = dscores[head]
        sums = []
        for label in range(32):
            chosen = jnp.where(ids == label, grid, 0.0)
            sums.append(jnp.sum(chosen, axis=0, keepdims=True))
        totals.append(jnp.sum(jnp.concatenate(sums, axis=0), axis=1, keepdims=True))
    place = lax.broadcasted_iota(jnp.int32, (32, 128), 1)
    for side in (0, 1):
        table = jnp.zeros((32, 128), F32)
        for head in range(3):
            table = jnp.where(place == head, totals[side * 3 + head], table)
        out[side] = table


def last_norm(
    xg, gains, part, recv, upper, gain_feed, gain_cross, tables, keep, send, small_keep,
    small_send,
):
    resid = own_rows(xg).astype(F32)
    back, gain = norm_back(part[...] + recv[...].astype(F32), resid, gain_row(gains, 0))
    total = jnp.transpose((upper[...] + back)[:, :384])

    def body(side):
        keep[...] = total[side * 192 : side * 192 + 192, :]
        send[...] = total[(1 - side) * 192 : (2 - side) * 192, :]

    each_side("col", body)
    rows = []
    for values in (gain, gain_cross[:1, :], gain_feed[:1, :]):
        rows += [values[:, at : at + 128] for at in (0, 128, 256)]
    rows = jnp.concatenate(rows + [jnp.zeros((7, 128), F32)], axis=0)
    small_keep[:16, :] = rows
    small_send[:16, :] = rows
    small_keep[16:, :] = tables[0]
    small_send[16:, :] = tables[1]


def finish_early(feed_keep, feed_recv, cross_keep, cross_recv, mine, send):
    for half, ref in ((0, mine), (1, send)):
        feed = feed_keep[half].astype(F32) + feed_recv[half].astype(F32)
        wide = cross_keep[half].astype(F32) + cross_recv[half].astype(F32)
        thin = cross_keep[2].astype(F32) + cross_recv[2].astype(F32)
        ref[:, :1024] = feed.astype(ref.dtype)
        ref[:, 1024:1408] = wide.astype(ref.dtype)
        ref[:, 1408:] = thin[:, half * 192 : half * 192 + 192].astype(ref.dtype)


def finish_self(keep, recv, mine, send):
    for half, ref in ((0, mine), (1, send)):
        wide = keep[half].astype(F32) + recv[half].astype(F32)
        thin = keep[2].astype(F32) + recv[2].astype(F32)
        ref[:, :384] = wide.astype(ref.dtype)
        ref[:, 384:] = thin[:, half * 192 : half * 192 + 192].astype(ref.dtype)


def place_columns(widths, mine, recv, *outs):
    def body(side):
        at = 0
        for width, out in zip(widths, outs):
            first = mine[:, at : at + width]
            second = recv[:, at : at + width].astype(F32)
            if side:
                first, second = second, first
            out[:, :width] = first
            out[:, width:] = second
            at += width

    each_side("row", body)


def place_early(mine, recv, *outs):
    place_columns((512, 512, 384, 192), mine, recv, *outs)


def place_self(mine, recv, *outs):
    place_columns((384, 192), mine, recv, *outs)


def finish_out(feed_keep, feed_recv, rest_keep, rest_recv, first, second):
    total = jnp.concatenate(
        [
            feed_keep[...].astype(F32) + feed_recv[...].astype(F32),
            rest_keep[...].astype(F32) + rest_recv[...].astype(F32),
        ],
        axis=0,
    ).astype(BF)
    swap = (lax.axis_index("dp") + lax.axis_index("row")) % 2

    def body(side):
        for ref, half in ((first, side), (second, 1 - side)):
            ref[...] = total[:, half * 384 : half * 384 + 384]

    for side in (0, 1):
        pl.when(swap == side)(lambda side=side: body(side))


def place_rows(first, second, *outs):
    def body(side):
        at = 0
        for out in outs:
            size = out.shape[0] // 2
            parts = [ref[at : at + size, :].astype(F32) for ref in (first, second)]
            if side:
                parts = parts[::-1]
            out[:size, :] = parts[0]
            out[size:, :] = parts[1]
            at += size

    each_side("row", body)


def build(replicas):
    bits = replicas.bit_length() - 1
    assert 1 << bits == replicas and replicas % 2 == 0

    def replica_swap(values, bit):
        return lax.ppermute(values, "dp", [(i, i ^ (1 << bit)) for i in range(replicas)])

    def scatter(values, axis, order):
        place = lax.axis_index("dp")
        shape = values.shape
        values = values.reshape(shape[:axis] + (2,) * bits + shape[axis + 1 :])
        left = list(range(bits - 1, -1, -1))
        for bit in order:
            at = axis + left.index(bit)
            left.remove(bit)
            mine = (place >> bit) & 1
            keep = lax.dynamic_index_in_dim(values, mine, at, keepdims=False)
            send = lax.dynamic_index_in_dim(values, 1 - mine, at, keepdims=False)
            recv = replica_swap(send, bit)
            values = (keep.astype(F32) + recv.astype(F32)).astype(BF)
        return keep, recv

    def spread(values):
        direct = row_swap(values)
        beside = replica_swap(direct, 0)
        parts = (direct, beside, replica_swap(direct, 1), replica_swap(beside, 1))
        return parts, tuple(col_swap(part) for part in parts)

    def core_sum(keep, send):
        return (keep.astype(F32) + col_swap(send).astype(F32)).astype(BF)

    def layer(
        hidden_in, encoder_states, token_segments, source_segments, buckets, gain_self, gain_cross,
        gain_feed, self_querykey, self_value, self_output, cross_query, cross_keyvalue,
        cross_output, gate_weight, up_weight, down_weight, bias_table, cotangent,
    ):
        core = lax.axis_index("col")
        forward = list(range(bits))
        backward = list(range(1, bits)) + [0]

        packed, s_keep, s_send = call(
            prep_self,
            [((192, 272), BF), ((384, 768), BF), ((96, 768), BF)],
            hidden_in.T, gain_self[None], gain_cross[None], gain_feed[None], self_querykey,
            self_value, self_output,
        )
        x_row = row_swap(packed)
        s_parts, s_peers = spread(s_send)
        s_other = col_swap(s_keep)
        table = jnp.pad(bias_table.T, ((0, 5), (0, 96)))
        peer_table = col_swap(table)
        bias, mask = call(
            masks, [((6, 128, 256), F32), ((128, 512), F32)],
            buckets, table, peer_table, token_segments, source_segments,
        )

        e_pack, c_keep, c_send = call(
            prep_cross,
            [((192, 768), BF), ((384, 768), BF), ((96, 768), BF)],
            encoder_states.T, cotangent.T, cross_query, cross_keyvalue, cross_output,
        )
        e_row = row_swap(e_pack)
        c_parts, c_peers = spread(c_send)
        c_other = col_swap(c_keep)

        f_keep, f_send, d_keep, d_send = call(
            prep_feed,
            [((384, 1024), BF), ((96, 1024), BF), ((512, 384), BF), ((128, 384), BF)],
            gate_weight, up_weight, down_weight,
        )
        d_parts, d_peers = spread(d_send)
        f_parts, f_peers = spread(f_send)
        f_other = col_swap(f_keep)
        d_other = col_swap(d_keep)

        part_shape = [((128, 768), F32), ((128, 768), BF)]
        matrix = [((384, 768), BF), ((384, 768), BF)]
        xg, gains, s_a1, s_b1, normed_self, ya, yb, self_mixed, self_lse, part, send = call(
            self_forward,
            [((256, 768), BF), ((16, 768), F32)] + matrix + [((256, 768), BF), ((256, 576), BF),
             ((256, 576), BF), ((128, 384), BF), ((6, 128, 1), F32)] + part_shape,
            packed, x_row, col_swap(packed), col_swap(x_row), s_keep, s_other,
            *s_parts, *s_peers, bias,
        )
        sw = (s_keep, s_a1, s_other, s_b1)
        recv = row_swap(send)
        ec, c_a1, c_b1, kva, kvb = call(
            encode_keys,
            [((768, 768), BF)] + matrix + [((512, 384), BF), ((512, 384), BF)],
            e_pack, e_row, col_swap(e_pack), col_swap(e_row), c_keep, c_other,
            *c_parts, *c_peers,
        )
        cw = (c_keep, c_a1, c_other, c_b1)
        resid_attn, normed_cross, cross_q, cross_mixed, cross_lse, part, send = call(
            cross_forward,
            [((128, 768), F32), ((128, 768), BF), ((128, 384), BF), ((128, 384), BF),
             ((6, 128, 1), F32)] + part_shape,
            xg, gains, part, recv, *cw, kva, kvb, mask,
        )
        recv = row_swap(send)
        f_a1, f_b1, d_a1, d_b1, upstream = call(
            feed_upstream,
            [((384, 1024), BF), ((384, 1024), BF), ((512, 384), BF), ((512, 384), BF),
             ((128, 1024), F32)],
            ec, d_keep, d_other, *f_parts, *f_peers, *d_parts, *d_peers,
        )
        dw = (d_keep, d_a1, d_other, d_b1)
        resid_cross, normed_feed, hidden, gate_delta, up_delta, part, send = call(
            feed_forward,
            [((128, 768), F32), ((128, 768), BF), ((128, 1024), BF), ((128, 1024), BF),
             ((128, 1024), BF)] + part_shape,
            xg, gains, resid_attn, part, recv, f_keep, f_a1, f_other, f_b1, upstream,
        )
        recv = row_swap(send)
        fi_keep, fi_send = call(
            feed_grads, [((768, 1024), BF), ((768, 1024), BF)],
            normed_feed, gate_delta, up_delta,
        )
        in_feed = core_sum(fi_keep, fi_send)
        fo_keep, fo_send, last_keep, last_send = call(
            feed_out,
            [((512, 768), BF), ((512, 768), BF), ((128, 384), F32), ((128, 384), BF)],
            hidden, ec, resid_cross, *dw,
        )
        out_feed = core_sum(fo_keep, fo_send)

        (grad_cross, upstream_cross, gain_feed_sum, cross_delta, dscores, probs, cross_dq, part,
         send) = call(
            cross_backward,
            [((128, 768), F32), ((128, 768), BF), ((8, 768), F32), ((128, 384), BF),
             ((6, 128, 512), BF), ((6, 128, 512), BF), ((128, 384), BF)] + part_shape,
            xg, gains, ec, part, recv, resid_cross, *cw, cross_q, kva, kvb, cross_lse, mask,
            cross_mixed,
        )
        recv = row_swap(send)
        ci_keep, ci_send, co_keep, co_send, enc_keep, enc_send = call(
            cross_grads,
            [((1152, 384), BF), ((1152, 384), BF), ((192, 768), BF), ((192, 768), BF),
             ((2, 192, 512), F32), ((2, 192, 512), BF)],
            ec, normed_cross, cross_q, cross_delta, dscores, probs, cross_dq, cross_mixed,
            upstream_cross, *cw,
        )
        in_cross = core_sum(ci_keep, ci_send)
        out_cross = core_sum(co_keep, co_send)

        (grad_attn, gain_cross_sum, dscores, dya, dyb, si_keep, si_send, so_keep, so_send) = call(
            self_backward,
            [((128, 768), F32), ((8, 768), F32), ((6, 128, 256), F32), ((256, 576), BF),
             ((256, 576), BF), ((1152, 384), BF), ((1152, 384), BF), ((192, 768), BF),
             ((192, 768), BF)],
            xg, gains, part, recv, grad_cross, resid_attn, *sw, normed_self, ya, yb, bias,
            self_lse, self_mixed,
        )
        in_self = core_sum(si_keep, si_send)
        out_self = core_sum(so_keep, so_send)
        keep, send = call(self_inputs, part_shape, dya, dyb, *sw)
        keep, send = call(self_sum, part_shape, keep, col_swap(send))
        recv = row_swap(send)
        (tables,) = call(table_sums, [((2, 32, 128), F32)], buckets, dscores)
        grad_keep, grad_send, small_keep, small_send = call(
            last_norm,
            [((192, 128), F32), ((192, 128), F32), ((48, 128), F32), ((48, 128), F32)],
            xg, gains, keep, recv, grad_attn, gain_feed_sum, gain_cross_sum, tables,
        )

        def join(mine, theirs):
            return jnp.where(
                core == 0,
                jnp.concatenate((mine, theirs), axis=1),
                jnp.concatenate((theirs, mine), axis=1),
            ).T

        grad_hidden = join(grad_keep, col_swap(grad_send))

        out_keep, out_send = call(
            last_out, [((192, 128), BF), ((192, 128), BF)],
            last_keep, row_swap(last_send),
        )
        hidden_out = join(out_keep, col_swap(out_send))

        enc = enc_keep + col_swap(enc_send).astype(F32)
        grad_encoder = (enc[0] + row_swap(enc[1].astype(BF)).astype(F32)).T

        total = small_keep + col_swap(small_send)
        for bit in range(bits):
            total = total + replica_swap(total, bit)
        gain_grads = lax.dynamic_slice_in_dim(total[:9].reshape(3, 384), core * 192, 192, axis=1)
        table_grad = total[16:, :3]

        per = 384 // replicas
        wide = 512 // replicas
        short = 192 // replicas

        def blocks_of(values):
            return values.reshape(replicas, values.shape[0] // replicas, 768)

        feed_pair = scatter(in_feed.reshape(2, replicas, per, 1024), 1, forward)
        out_pair = scatter(blocks_of(out_feed), 0, backward)
        cross_pair = scatter(in_cross.reshape(3, replicas, per, 384), 1, forward)
        self_pair = scatter(in_self.reshape(3, replicas, per, 384), 1, forward)
        rest_pair = scatter(
            jnp.concatenate((blocks_of(out_cross), blocks_of(out_self)), axis=1), 0, forward
        )

        mine, send = call(
            finish_early, [((per, 1600), F32), ((per, 1600), BF)],
            *feed_pair, *cross_pair,
        )
        gate_grad, up_grad, keyvalue_grad, crossquery_grad = call(
            place_early,
            [((per, 1024), F32), ((per, 1024), F32), ((per, 768), F32), ((per, 384), F32)],
            mine, row_swap(send),
        )
        mine, send = call(
            finish_self, [((per, 576), F32), ((per, 576), BF)], *self_pair
        )
        querykey_grad, value_grad = call(
            place_self,
            [((per, 768), F32), ((per, 384), F32)],
            mine, row_swap(send),
        )

        sends = call(
            finish_out, [((wide + 2 * short, 384), BF)] * 2, *out_pair, *rest_pair
        )
        got = []
        for shift in (0, 1):
            moves = []
            for source in range(2 * replicas):
                replica, side = divmod(source, 2)
                block = side * replicas + replica
                moves.append((source, (block // 2) * 2 + ((block % 2) ^ shift)))
            got.append(lax.ppermute(sends[shift], ("dp", "row"), moves))
        down_grad, crossout_grad, output_grad = call(
            place_rows,
            [((2 * wide, 384), F32), ((2 * short, 384), F32), ((2 * short, 384), F32)], *got,
        )

        return (
            hidden_out, grad_hidden, grad_encoder, querykey_grad, value_grad, output_grad,
            crossquery_grad, keyvalue_grad, crossout_grad, gate_grad, up_grad, down_grad,
            gain_grads[0], gain_grads[1], gain_grads[2], table_grad,
        )

    return layer


def solution(mesh):
    tokens = P("dp", ("row", "col"))
    inward = P("row", "col")
    outward = P("col", "row")
    features = P(("row", "col"))
    inward_grad = P(("row", "dp"), "col")
    outward_grad = P(("col", "dp"), "row")
    bias = P(None, ("col", "row"))
    return jax.shard_map(
        build(mesh.shape["dp"]),
        mesh=mesh,
        in_specs=(
            tokens, tokens, P("dp", None), P("dp", None), P(), features, features, features,
            inward, inward, outward, inward, inward, outward, inward, inward, outward, bias,
            tokens,
        ),
        out_specs=(
            tokens, tokens, tokens, inward_grad, inward_grad, outward_grad, inward_grad,
            inward_grad, outward_grad, inward_grad, inward_grad, outward_grad, features, features,
            features, bias,
        ),
        check_vma=False,
    )
```

```python
import jax
import jax.numpy as jnp
from jax import lax
from jax.experimental import pallas as pl
from jax.experimental.pallas import tpu as pltpu
from jax.sharding import PartitionSpec as P


BF = jnp.bfloat16
F32 = jnp.float32
EPS = 1e-06
ROOT = 0.7978845608028654
CUBIC = 0.044715
MASKED = -1e30
SWAP = [(0, 1), (1, 0)]


def nn(left, right):
    return jnp.dot(left, right, preferred_element_type=F32)


def nt(left, right):
    return lax.dot_general(left, right, (((1,), (1,)), ((), ())), preferred_element_type=F32)


def tn(left, right):
    return lax.dot_general(left, right, (((0,), (0,)), ((), ())), preferred_element_type=F32)


def far(values):
    return pltpu.with_memory_space_constraint(values, pltpu.HBM)


def call(kernel, outs, *args, hbm=()):
    flat = [
        (pltpu.HBM if at in hbm else jax.ShapeDtypeStruct)(shape, dtype)
        for at, (shape, dtype) in enumerate(outs)
    ]
    space = pl.BlockSpec(memory_space=pltpu.VMEM)
    got = pl.pallas_call(
        kernel,
        out_shape=flat,
        in_specs=[space] * len(args),
        out_specs=[space] * len(flat),
        compiler_params=pltpu.CompilerParams(vmem_limit_bytes=16 * 1024 * 1024),
    )(*args)
    return [far(out) if at in hbm else out for at, out in enumerate(got)]


def row_swap(values):
    return lax.ppermute(values, "row", SWAP)


def col_swap(values):
    return lax.ppermute(values, "col", SWAP)


def own_rows(ref, base=0):
    half = 128
    start = base + lax.axis_index("col") * half
    return ref[pl.ds(pl.multiple_of(start, 16), half), :]


def each_side(axis, body):
    index = lax.axis_index(axis)
    for side in (0, 1):
        pl.when(index == side)(lambda side=side: body(side))


def swapped(ref, left, right):
    width = left.shape[1]
    ref[:, :width] = right.astype(BF)
    ref[:, width:] = left.astype(BF)


def each_replica(body):
    for part in range(4):
        pl.when(lax.axis_index("dp") % 4 == part)(lambda part=part: body(part))


def weight_parts(keep_body, send_body):
    def of_row(side):
        keep_body(side)
        each_replica(lambda part: send_body(1 - side, part))

    each_side("row", of_row)


def keep_cols(src, keep, at, width, side):
    keep[:, at : at + width] = src[:, side * width : (side + 1) * width]


def send_cols(src, send, at, width, side, part):
    rows = src.shape[0] // 4
    send[:, at : at + width] = src[
        part * rows : (part + 1) * rows, side * width : (side + 1) * width
    ]


def keep_out(src, keep, at, side):
    rows = src.shape[0] // 2
    width = src.shape[1] // 2
    for block in (0, 1):
        keep[block * rows : (block + 1) * rows, at : at + width] = src[
            side * rows : (side + 1) * rows, block * width : (block + 1) * width
        ]


def send_out(src, send, at, side, part):
    rows = src.shape[0] // 4
    width = src.shape[1] // 2
    start = side * 2 * rows + part % 2 * rows
    send[:, at : at + width] = src[
        start : start + rows, part // 2 * width : (part // 2 + 1) * width
    ]


def join_parts(parts, out):
    rows = parts[0].shape[0]
    place = lax.axis_index("dp") % 4
    for away, part in enumerate(parts):
        start = jnp.bitwise_xor(place, away) * rows
        out[pl.ds(pl.multiple_of(start, 16), rows), :] = part[...]


def assemble(own, recv, own_peer, recv_peer):
    core = lax.axis_index("col")
    first = core == 0
    quarters = (
        jnp.where(first, own[...], own_peer[...]),
        jnp.where(first, own_peer[...], own[...]),
        jnp.where(first, recv[...], recv_peer[...]),
        jnp.where(first, recv_peer[...], recv[...]),
    )
    return jnp.concatenate(quarters, axis=0)


def pack_three(wide, narrow, out, keep, send):
    def keep_body(side):
        keep_cols(wide, keep, 0, 384, side)
        keep_cols(narrow, keep, 384, 192, side)
        keep_out(out, keep, 576, side)

    def send_body(side, part):
        send_cols(wide, send, 0, 384, side, part)
        send_cols(narrow, send, 384, 192, side, part)
        send_out(out, send, 576, side, part)

    weight_parts(keep_body, send_body)


def prep_self(hidden, gs, gc, gf, qk, v, wo, packed, keep, send):
    tokens = hidden.shape[1]
    packed[:, :tokens] = hidden[...]
    gains = jnp.concatenate([gs[...], gc[...], gf[...]], axis=0)
    high = gains.astype(BF)
    low = (gains - high.astype(F32)).astype(BF)
    rows = jnp.concatenate(
        [high.astype(F32), low.astype(F32), jnp.zeros((10, gains.shape[1]), F32)], axis=0
    ).astype(BF)
    line = lax.broadcasted_iota(jnp.int32, (16, 16), 0)
    place = lax.broadcasted_iota(jnp.int32, (16, 16), 1)
    packed[:, tokens:] = tn(rows, jnp.where(line == place, 1.0, 0.0).astype(BF)).astype(BF)

    pack_three(qk, v, wo, keep, send)


def prep_cross(enc, cot, q, kv, wo, packed, keep, send):
    packed[:, : enc.shape[1]] = enc[...]
    packed[:, enc.shape[1] :] = cot[...]

    pack_three(kv, q, wo, keep, send)


def prep_feed(gate, up, down, keep, send, keep_down, send_down):
    def keep_body(side):
        keep_cols(gate, keep, 0, 512, side)
        keep_cols(up, keep, 512, 512, side)
        keep_down[...] = down[side * 512 : (side + 1) * 512, :]

    def send_body(side, part):
        send_cols(gate, send, 0, 512, side, part)
        send_cols(up, send, 512, 512, side, part)
        at = side * 512 + part * 128
        send_down[...] = down[at : at + 128, :]

    weight_parts(keep_body, send_body)


def masks(buckets, table, peer_table, segment, source, bias_out, cross_out):
    core = lax.axis_index("col")
    ids = own_rows(buckets)
    rows, cols = ids.shape
    line = lax.broadcasted_iota(jnp.int32, (rows, cols), 0) + core * rows
    place = lax.broadcasted_iota(jnp.int32, (rows, cols), 1)
    keys = segment[...]
    mine = jnp.sum(
        jnp.where(place == line, jnp.broadcast_to(keys, (rows, cols)).astype(F32), 0.0),
        axis=1,
        keepdims=True,
    )
    allowed = (place <= line) & (keys.astype(F32) == mine)
    for head in range(6):
        ref = table if head < 3 else peer_table
        entries = jnp.broadcast_to(ref[head % 3 : head % 3 + 1, :], (rows, 128))
        parts = [
            jnp.take_along_axis(
                entries, ids[:, at : at + 128], axis=1, mode="promise_in_bounds"
            )
            for at in range(0, cols, 128)
        ]
        bias_out[head] = jnp.where(allowed, jnp.concatenate(parts, axis=1), MASKED)
    cross_out[...] = jnp.where(source[...].astype(F32) == mine, 0.0, MASKED)


def gain_row(gains, which):
    return gains[which : which + 1, :]


def norm(resid, gain):
    scale = lax.rsqrt(jnp.mean(resid * resid, axis=1, keepdims=True) + EPS)
    return resid * scale * gain, scale


def norm_back(upstream, resid, gain):
    scale = lax.rsqrt(jnp.mean(resid * resid, axis=1, keepdims=True) + EPS)
    normed = resid * scale
    scaled = upstream * gain
    grad = scale * (scaled - normed * jnp.mean(scaled * normed, axis=1, keepdims=True))
    return grad, jnp.sum(upstream * normed, axis=0, keepdims=True)


def project(left, top, bottom, at, width):
    return nn(left[:, :384], top[:, at : at + width]) + nn(left[:, 384:], bottom[:, at : at + width])


def softmax(scores):
    top = jnp.max(scores, axis=1, keepdims=True)
    weights = jnp.exp(scores - top)
    total = jnp.sum(weights, axis=1, keepdims=True)
    return (weights * (1.0 / total)).astype(BF), top + jnp.log(total)


def out_project(mixed, a0, a1, b0, b1, keep, send):
    first, second = mixed[:, :192], mixed[:, 192:]
    parts = []
    for a, b in ((a0, b0), (a1, b1)):
        for block in (0, 1):
            lines = slice(block * 192, (block + 1) * 192)
            parts.append(nn(first, a[lines, 576:]) + nn(second, b[lines, 576:]))
    mine = jnp.concatenate(parts[:2], axis=1)
    theirs = jnp.concatenate(parts[2:], axis=1)
    keep[:, :384] = mine
    keep[:, 384:] = theirs
    swapped(send, mine, theirs)


def out_back(upstream, w0, w1):
    total = None
    for half, w in ((0, w0), (1, w1)):
        for block in (0, 1):
            at = half * 384 + block * 192
            term = nt(upstream[:, at : at + 192], w[block * 192 : (block + 1) * 192, 576:])
            total = term if total is None else total + term
    return total


def self_forward(
    own, recv, own_peer, recv_peer, a0, b0, p0, p1, p2, p3, q0, q1, q2, q3, bias, x_out, gains_out, a1, b1, normed_out, ya, yb, mixed_out, lse_out, keep, send,
):
    join_parts((p0, p1, p2, p3), a1)
    join_parts((q0, q1, q2, q3), b1)
    tokens = normed_out.shape[0]
    whole = assemble(own, recv, own_peer, recv_peer).astype(F32)
    resid = jnp.transpose(whole[:, :tokens])
    x_out[...] = resid.astype(BF)
    parts = whole[:, tokens:].astype(BF)
    line = lax.broadcasted_iota(jnp.int32, (16, 16), 0)
    place = lax.broadcasted_iota(jnp.int32, (16, 16), 1)
    chosen = (line == place) | ((line == place - 3) & (place < 6))
    chosen = jnp.where(chosen & (line < 3), 1.0, 0.0).astype(BF)
    gains_out[...] = nt(chosen, parts)
    normed = norm(resid, gain_row(gains_out, 0))[0].astype(BF)
    normed_out[...] = normed
    ya[...] = project(normed, a0, a1, 0, 576).astype(BF)
    yb[...] = project(normed, b0, b1, 0, 576).astype(BF)
    mixed = []
    for head in range(6):
        y = ya if head < 3 else yb
        at = (head % 3) * 128
        mine = own_rows(y)
        scores = nt(mine[:, at : at + 64], y[:, at + 64 : at + 128]) + bias[head]
        probs, lse = softmax(scores)
        lse_out[head] = lse
        at = 384 + (head % 3) * 64
        mixed.append(nn(probs, y[:, at : at + 64]))
    mixed = jnp.concatenate(mixed, axis=1).astype(BF)
    mixed_out[...] = mixed
    out_project(mixed, a0, a1, b0, b1, keep, send)


def encode_keys(
    own, recv, own_peer, recv_peer, a0, b0, p0, p1, p2, p3, q0, q1, q2, q3, ec, a1, b1, kva, kvb,
):
    join_parts((p0, p1, p2, p3), a1)
    join_parts((q0, q1, q2, q3), b1)
    rows = kva.shape[0]
    whole = assemble(own, recv, own_peer, recv_peer).astype(F32)
    ec[...] = jnp.transpose(whole).astype(BF)
    enc = ec[:rows, :]
    kva[...] = project(enc, a0, a1, 0, 384).astype(BF)
    kvb[...] = project(enc, b0, b1, 0, 384).astype(BF)


def cross_forward(
    xg, gains, part, recv, a0, a1, b0, b1, kva, kvb, mask, resid_out, normed_out, q_out, mixed_out,
    lse_out, keep, send,
):
    resid = own_rows(xg).astype(F32) + part[...] + recv[...].astype(F32)
    resid_out[...] = resid
    normed = norm(resid, gain_row(gains, 1))[0].astype(BF)
    normed_out[...] = normed
    queries = jnp.concatenate(
        [project(normed, a0, a1, 384, 192), project(normed, b0, b1, 384, 192)], axis=1
    ).astype(BF)
    q_out[...] = queries
    mixed = []
    for head in range(6):
        kv = kva if head < 3 else kvb
        at = (head % 3) * 128
        scores = nt(queries[:, head * 64 : head * 64 + 64], kv[:, at : at + 64]) + mask[...]
        probs, lse = softmax(scores)
        lse_out[head] = lse
        mixed.append(nn(probs, kv[:, at + 64 : at + 128]))
    mixed = jnp.concatenate(mixed, axis=1).astype(BF)
    mixed_out[...] = mixed
    out_project(mixed, a0, a1, b0, b1, keep, send)


def feed_upstream(ec, da0, db0, *refs):
    parts, (fa1, fb1, da1, db1, out) = refs[:16], refs[16:]
    for at, ref in enumerate((fa1, fb1, da1, db1)):
        join_parts(parts[at * 4 : at * 4 + 4], ref)
    cot = own_rows(ec, ec.shape[0] - 256)
    out[:, :512] = nt(cot[:, :384], da0[...]) + nt(cot[:, 384:], da1[...])
    out[:, 512:] = nt(cot[:, :384], db0[...]) + nt(cot[:, 384:], db1[...])


def feed_forward(
    xg, gains, prior, part, recv, fa0, fa1, fb0, fb1, upstream, resid_out, normed_out, hidden_out,
    gate_out, up_out, keep, send,
):
    resid = prior[...] + part[...] + recv[...].astype(F32)
    resid_out[...] = resid
    normed = norm(resid, gain_row(gains, 2))[0].astype(BF)
    normed_out[...] = normed
    deltas = []
    for side, (w0, w1) in enumerate(((fa0, fa1), (fb0, fb1))):
        lanes = slice(side * 512, side * 512 + 512)
        gate = project(normed, w0, w1, 0, 512)
        up = project(normed, w0, w1, 512, 512)
        inner = jnp.tanh(ROOT * (gate + CUBIC * gate * gate * gate))
        gelu = 0.5 * gate * (1.0 + inner)
        slope = 0.5 * (1.0 + inner) + 0.5 * gate * (1.0 - inner * inner) * ROOT * (
            1.0 + 3.0 * CUBIC * gate * gate
        )
        grad = upstream[:, lanes]
        hidden_out[:, lanes] = (gelu * up).astype(BF)
        gate_delta = (grad * up * slope).astype(BF)
        up_delta = (grad * gelu).astype(BF)
        gate_out[:, lanes] = gate_delta
        up_out[:, lanes] = up_delta
        deltas.append((gate_delta, up_delta))
    (ga, ua), (gb, ub) = deltas
    mine = nt(ga, fa0[:, :512]) + nt(ua, fa0[:, 512:]) + nt(gb, fb0[:, :512]) + nt(ub, fb0[:, 512:])
    theirs = (
        nt(ga, fa1[:, :512]) + nt(ua, fa1[:, 512:]) + nt(gb, fb1[:, :512]) + nt(ub, fb1[:, 512:])
    )
    keep[:, :384] = mine
    keep[:, 384:] = theirs
    swapped(send, mine, theirs)


def feed_grads(normed, gate, up, in_keep, in_send):
    left = normed[...]
    for ref, lanes in ((in_send, slice(512, 1024)), (in_keep, slice(0, 512))):
        ref[:, :512] = tn(left, gate[:, lanes]).astype(BF)
        ref[:, 512:] = tn(left, up[:, lanes]).astype(BF)


def feed_out(hidden, ec, resid, da0, da1, db0, db1, out_keep, out_send, last_keep, last_send):
    cot = own_rows(ec, ec.shape[0] - 256)
    out_send[...] = tn(hidden[:, 512:], cot).astype(BF)
    out_keep[...] = tn(hidden[:, :512], cot).astype(BF)
    last_send[...] = (nn(hidden[:, :512], da1[...]) + nn(hidden[:, 512:], db1[...])).astype(BF)
    last_keep[...] = (
        nn(hidden[:, :512], da0[...]) + nn(hidden[:, 512:], db0[...]) + resid[:, :384]
    )


def last_out(part, recv, keep, send):
    total = jnp.transpose(part[...] + recv[...].astype(F32)).astype(BF)

    def body(side):
        keep[...] = total[side * 192 : side * 192 + 192, :]
        send[...] = total[(1 - side) * 192 : (2 - side) * 192, :]

    each_side("col", body)


def store_grads(ref, left, wide, narrow, narrow_left):
    ref[:768, :] = tn(left, wide).astype(BF)
    thin = tn(narrow_left, narrow).astype(BF)
    ref[768:, :192] = thin[:384, :]
    ref[768:, 192:] = thin[384:, :]


def cross_backward(
    xg, gains, ec, part, recv, resid_in, a0, a1, b0, b1, q, kva, kvb, lse, mask, mixed, resid_out,
    upstream_out, gain_out, delta_out, dscores_out, probs_out, dq_out, keep, send,
):
    back, gain = norm_back(part[...] + recv[...].astype(F32), resid_in[...], gain_row(gains, 2))
    gain_out[...] = jnp.broadcast_to(gain, gain_out.shape)
    resid = own_rows(ec, ec.shape[0] - 256).astype(F32) + back
    resid_out[...] = resid
    upstream = resid.astype(BF)
    upstream_out[...] = upstream
    delta = jnp.concatenate(
        [out_back(upstream, a0, a1), out_back(upstream, b0, b1)], axis=1
    ).astype(BF)
    delta_out[...] = delta
    grads = []
    for head in range(6):
        kv = kva if head < 3 else kvb
        at = (head % 3) * 128
        lanes = slice(head * 64, head * 64 + 64)
        scores = nt(q[:, lanes], kv[:, at : at + 64]) + mask[...]
        probs = jnp.exp(scores - lse[head])
        probs_out[head] = probs.astype(BF)
        drift = nt(delta[:, lanes], kv[:, at + 64 : at + 128])
        centre = jnp.sum(
            delta[:, lanes].astype(F32) * mixed[:, lanes].astype(F32), axis=1, keepdims=True
        )
        low = (probs * (drift - centre)).astype(BF)
        dscores_out[head] = low
        grads.append(nn(low, kv[:, at : at + 64]))
    grads = jnp.concatenate(grads, axis=1).astype(BF)
    dq_out[...] = grads
    first, second = grads[:, :192], grads[:, 192:]
    mine = nt(first, a0[:, 384:576]) + nt(second, b0[:, 384:576])
    theirs = nt(first, a1[:, 384:576]) + nt(second, b1[:, 384:576])
    keep[:, :384] = mine
    keep[:, 384:] = theirs
    swapped(send, mine, theirs)


def cross_grads(
    ec, normed, q, delta, dscores, probs, dq, mixed, upstream, a0, a1, b0, b1, in_keep, in_send,
    out_keep, out_send, enc_keep, enc_send,
):
    rows = ec.shape[0] - 256
    enc = ec[:rows, :]
    left = normed[...]
    both = []
    for first in (0, 3):
        parts = []
        for head in range(first, first + 3):
            lanes = slice(head * 64, head * 64 + 64)
            parts.append(tn(dscores[head], q[:, lanes]))
            parts.append(tn(probs[head], delta[:, lanes]))
        both.append(jnp.concatenate(parts, axis=1).astype(BF))
    for ref, side in ((in_send, 1), (in_keep, 0)):
        store_grads(ref, enc, both[side], dq[:, side * 192 : side * 192 + 192], left)
    out_send[...] = tn(mixed[:, 192:], upstream[...]).astype(BF)
    out_keep[...] = tn(mixed[:, :192], upstream[...]).astype(BF)
    for half, (a, b) in enumerate(((a0, b0), (a1, b1))):
        total = nt(a[:, :384], both[0]) + nt(b[:, :384], both[1])

        def body(side, half=half, total=total):
            enc_keep[half] = total[side * 192 : side * 192 + 192, :]
            enc_send[half] = total[(1 - side) * 192 : (2 - side) * 192, :].astype(BF)

        each_side("col", body)


def self_backward(
    xg, gains, part, recv, upper, resid_in, a0, a1, b0, b1, normed, ya, yb, bias, lse, mixed, resid_out,
    gain_out, dscores_out, dya, dyb, in_keep, in_send, out_keep, out_send,
):
    back, gain = norm_back(part[...] + recv[...].astype(F32), resid_in[...], gain_row(gains, 1))
    gain_out[...] = jnp.broadcast_to(gain, gain_out.shape)
    resid = upper[...] + back
    resid_out[...] = resid
    upstream = resid.astype(BF)
    delta = jnp.concatenate(
        [out_back(upstream, a0, a1), out_back(upstream, b0, b1)], axis=1
    ).astype(BF)
    out_send[...] = tn(mixed[:, 192:], upstream).astype(BF)
    out_keep[...] = tn(mixed[:, :192], upstream).astype(BF)
    core = lax.axis_index("col").astype(F32)
    for y, dy, first in ((yb, dyb, 3), (ya, dya, 0)):
        mine = own_rows(y)
        pairs, values = [], []
        for head in range(first, first + 3):
            at = (head % 3) * 128
            vat = 384 + (head % 3) * 64
            lanes = slice(head * 64, head * 64 + 64)
            queries = mine[:, at : at + 64]
            scores = nt(queries, y[:, at + 64 : at + 128]) + bias[head]
            probs = jnp.exp(scores - lse[head])
            up = delta[:, lanes]
            drift = nt(up, y[:, vat : vat + 64])
            centre = jnp.sum(
                up.astype(F32) * mixed[:, lanes].astype(F32), axis=1, keepdims=True
            )
            dscores = probs * (drift - centre)
            dscores_out[head] = dscores
            low = dscores.astype(BF)
            dq = nn(low, y[:, at + 64 : at + 128])
            dq = jnp.concatenate([dq * (1.0 - core), dq * core], axis=0)
            pairs.append(jnp.concatenate([dq, tn(low, queries)], axis=1))
            values.append(tn(probs.astype(BF), up))
        dy[...] = jnp.concatenate(pairs + values, axis=1).astype(BF)
    left = normed[...]
    for ref, dy in ((in_send, dyb), (in_keep, dya)):
        store_grads(ref, left, dy[:, :384], dy[:, 384:], left)


def self_inputs(dya, dyb, a0, a1, b0, b1, keep, send):
    da, db = dya[...], dyb[...]
    totals = [nt(da, a[:, :576]) + nt(db, b[:, :576]) for a, b in ((a0, b0), (a1, b1))]

    def body(side):
        mine = slice(side * 128, side * 128 + 128)
        theirs = slice((1 - side) * 128, (1 - side) * 128 + 128)
        for at, total in ((0, totals[0]), (384, totals[1])):
            keep[:, at : at + 384] = total[mine, :]
            send[:, at : at + 384] = total[theirs, :].astype(BF)

    each_side("col", body)


def self_sum(part, other, keep, send):
    total = part[...] + other[...].astype(F32)
    keep[...] = total
    swapped(send, total[:, :384], total[:, 384:])


def table_sums(buckets, dscores, out):
    ids = own_rows(buckets)
    totals = []
    for head in range(6):
        grid = dscores[head]
        sums = []
        for label in range(32):
            chosen = jnp.where(ids == label, grid, 0.0)
            sums.append(jnp.sum(chosen, axis=0, keepdims=True))
        totals.append(jnp.sum(jnp.concatenate(sums, axis=0), axis=1, keepdims=True))
    place = lax.broadcasted_iota(jnp.int32, (32, 128), 1)
    for side in (0, 1):
        table = jnp.zeros((32, 128), F32)
        for head in range(3):
            table = jnp.where(place == head, totals[side * 3 + head], table)
        out[side] = table


def last_norm(
    xg, gains, part, recv, upper, gain_feed, gain_cross, tables, keep, send, small_keep,
    small_send,
):
    resid = own_rows(xg).astype(F32)
    back, gain = norm_back(part[...] + recv[...].astype(F32), resid, gain_row(gains, 0))
    total = jnp.transpose((upper[...] + back)[:, :384])

    def body(side):
        keep[...] = total[side * 192 : side * 192 + 192, :]
        send[...] = total[(1 - side) * 192 : (2 - side) * 192, :]

    each_side("col", body)
    rows = []
    for values in (gain, gain_cross[:1, :], gain_feed[:1, :]):
        rows += [values[:, at : at + 128] for at in (0, 128, 256)]
    rows = jnp.concatenate(rows + [jnp.zeros((7, 128), F32)], axis=0)
    small_keep[:16, :] = rows
    small_send[:16, :] = rows
    small_keep[16:, :] = tables[0]
    small_send[16:, :] = tables[1]


def finish_early(feed_keep, feed_recv, cross_keep, cross_recv, mine, send):
    for half, ref in ((0, mine), (1, send)):
        feed = feed_keep[half].astype(F32) + feed_recv[half].astype(F32)
        wide = cross_keep[half].astype(F32) + cross_recv[half].astype(F32)
        thin = cross_keep[2].astype(F32) + cross_recv[2].astype(F32)
        ref[:, :1024] = feed.astype(ref.dtype)
        ref[:, 1024:1408] = wide.astype(ref.dtype)
        ref[:, 1408:] = thin[:, half * 192 : half * 192 + 192].astype(ref.dtype)


def finish_self(keep, recv, mine, send):
    for half, ref in ((0, mine), (1, send)):
        wide = keep[half].astype(F32) + recv[half].astype(F32)
        thin = keep[2].astype(F32) + recv[2].astype(F32)
        ref[:, :384] = wide.astype(ref.dtype)
        ref[:, 384:] = thin[:, half * 192 : half * 192 + 192].astype(ref.dtype)


def place_columns(widths, mine, recv, *outs):
    def body(side):
        at = 0
        for width, out in zip(widths, outs):
            first = mine[:, at : at + width]
            second = recv[:, at : at + width].astype(F32)
            if side:
                first, second = second, first
            out[:, :width] = first
            out[:, width:] = second
            at += width

    each_side("row", body)


def place_early(mine, recv, *outs):
    place_columns((512, 512, 384, 192), mine, recv, *outs)


def place_self(mine, recv, *outs):
    place_columns((384, 192), mine, recv, *outs)


def finish_out(feed_keep, feed_recv, rest_keep, rest_recv, first, second):
    total = jnp.concatenate(
        [
            feed_keep[...].astype(F32) + feed_recv[...].astype(F32),
            rest_keep[...].astype(F32) + rest_recv[...].astype(F32),
        ],
        axis=0,
    ).astype(BF)
    swap = (lax.axis_index("dp") + lax.axis_index("row")) % 2

    def body(side):
        for ref, half in ((first, side), (second, 1 - side)):
            ref[...] = total[:, half * 384 : half * 384 + 384]

    for side in (0, 1):
        pl.when(swap == side)(lambda side=side: body(side))


def place_rows(first, second, *outs):
    def body(side):
        at = 0
        for out in outs:
            size = out.shape[0] // 2
            parts = [ref[at : at + size, :].astype(F32) for ref in (first, second)]
            if side:
                parts = parts[::-1]
            out[:size, :] = parts[0]
            out[size:, :] = parts[1]
            at += size

    each_side("row", body)


def build(replicas):
    bits = replicas.bit_length() - 1
    assert 1 << bits == replicas and replicas % 2 == 0

    def replica_swap(values, bit):
        return lax.ppermute(values, "dp", [(i, i ^ (1 << bit)) for i in range(replicas)])

    def scatter(values, axis, order):
        place = lax.axis_index("dp")
        shape = values.shape
        values = values.reshape(shape[:axis] + (2,) * bits + shape[axis + 1 :])
        left = list(range(bits - 1, -1, -1))
        for bit in order:
            at = axis + left.index(bit)
            left.remove(bit)
            mine = (place >> bit) & 1
            keep = lax.dynamic_index_in_dim(values, mine, at, keepdims=False)
            send = lax.dynamic_index_in_dim(values, 1 - mine, at, keepdims=False)
            recv = replica_swap(send, bit)
            values = (keep.astype(F32) + recv.astype(F32)).astype(BF)
        return keep, recv

    def spread(values):
        direct = row_swap(values)
        beside = replica_swap(direct, 0)
        parts = (direct, beside, replica_swap(direct, 1), replica_swap(beside, 1))
        return parts, tuple(col_swap(part) for part in parts)

    def core_sum(keep, send):
        return (keep.astype(F32) + col_swap(send).astype(F32)).astype(BF)

    def layer(
        hidden_in, encoder_states, token_segments, source_segments, buckets, gain_self, gain_cross,
        gain_feed, self_querykey, self_value, self_output, cross_query, cross_keyvalue,
        cross_output, gate_weight, up_weight, down_weight, bias_table, cotangent,
    ):
        core = lax.axis_index("col")
        (buckets, self_querykey, self_value, self_output, cross_query, cross_keyvalue,
         cross_output, gate_weight, up_weight, down_weight, token_segments, source_segments) = map(
            far,
            (buckets, self_querykey, self_value, self_output, cross_query, cross_keyvalue,
             cross_output, gate_weight, up_weight, down_weight, token_segments, source_segments),
        )
        forward = list(range(bits))
        backward = list(range(1, bits)) + [0]

        packed, s_keep, s_send = call(
            prep_self,
            [((192, 272), BF), ((384, 768), BF), ((96, 768), BF)],
            far(hidden_in.T), far(gain_self[None]), far(gain_cross[None]), far(gain_feed[None]), self_querykey,
            self_value, self_output,
        )
        x_row = row_swap(packed)
        s_parts, s_peers = spread(s_send)
        s_other = col_swap(s_keep)
        table = jnp.pad(bias_table.T, ((0, 5), (0, 96)))
        peer_table = col_swap(table)
        bias, mask = call(
            masks, [((6, 128, 256), F32), ((128, 512), F32)],
            buckets, table, peer_table, token_segments, source_segments, hbm=(0, 1),
        )

        e_pack, c_keep, c_send = call(
            prep_cross,
            [((192, 768), BF), ((384, 768), BF), ((96, 768), BF)],
            far(encoder_states.T), far(cotangent.T), cross_query, cross_keyvalue, cross_output,
        )
        e_row = row_swap(e_pack)
        c_parts, c_peers = spread(c_send)
        c_other = col_swap(c_keep)

        f_keep, f_send, d_keep, d_send = call(
            prep_feed,
            [((384, 1024), BF), ((96, 1024), BF), ((512, 384), BF), ((128, 384), BF)],
            gate_weight, up_weight, down_weight,
        )
        d_parts, d_peers = spread(d_send)
        f_parts, f_peers = spread(f_send)
        f_other = col_swap(f_keep)
        d_other = col_swap(d_keep)

        part_shape = [((128, 768), F32), ((128, 768), BF)]
        matrix = [((384, 768), BF), ((384, 768), BF)]
        xg, gains, s_a1, s_b1, normed_self, ya, yb, self_mixed, self_lse, part, send = call(
            self_forward,
            [((256, 768), BF), ((16, 768), F32)] + matrix + [((256, 768), BF), ((256, 576), BF),
             ((256, 576), BF), ((128, 384), BF), ((6, 128, 1), F32)] + part_shape,
            packed, x_row, col_swap(packed), col_swap(x_row), s_keep, s_other,
            *s_parts, *s_peers, bias, hbm=(0, 1, 2, 3, 4, 5, 6, 7, 8),
        )
        sw = (far(s_keep), s_a1, far(s_other), s_b1)
        recv = row_swap(send)
        ec, c_a1, c_b1, kva, kvb = call(
            encode_keys,
            [((768, 768), BF)] + matrix + [((512, 384), BF), ((512, 384), BF)],
            e_pack, e_row, col_swap(e_pack), col_swap(e_row), c_keep, c_other,
            *c_parts, *c_peers, hbm=(0, 1, 2, 3, 4),
        )
        cw = (far(c_keep), c_a1, far(c_other), c_b1)
        resid_attn, normed_cross, cross_q, cross_mixed, cross_lse, part, send = call(
            cross_forward,
            [((128, 768), F32), ((128, 768), BF), ((128, 384), BF), ((128, 384), BF),
             ((6, 128, 1), F32)] + part_shape,
            xg, gains, part, recv, *cw, kva, kvb, mask, hbm=(0, 1, 2, 3, 4),
        )
        recv = row_swap(send)
        f_a1, f_b1, d_a1, d_b1, upstream = call(
            feed_upstream,
            [((384, 1024), BF), ((384, 1024), BF), ((512, 384), BF), ((512, 384), BF),
             ((128, 1024), F32)],
            ec, d_keep, d_other, *f_parts, *f_peers, *d_parts, *d_peers, hbm=(2, 3),
        )
        dw = (far(d_keep), d_a1, far(d_other), d_b1)
        resid_cross, normed_feed, hidden, gate_delta, up_delta, part, send = call(
            feed_forward,
            [((128, 768), F32), ((128, 768), BF), ((128, 1024), BF), ((128, 1024), BF),
             ((128, 1024), BF)] + part_shape,
            xg, gains, resid_attn, part, recv, f_keep, f_a1, f_other, f_b1, upstream, hbm=(0, 2),
        )
        recv = row_swap(send)
        fi_keep, fi_send = call(
            feed_grads, [((768, 1024), BF), ((768, 1024), BF)],
            normed_feed, gate_delta, up_delta,)
        in_feed = core_sum(fi_keep, fi_send)
        fo_keep, fo_send, last_keep, last_send = call(
            feed_out,
            [((512, 768), BF), ((512, 768), BF), ((128, 384), F32), ((128, 384), BF)],
            hidden, ec, resid_cross, *dw, hbm=(2,),
        )
        out_feed = core_sum(fo_keep, fo_send)

        (grad_cross, upstream_cross, gain_feed_sum, cross_delta, dscores, probs, cross_dq, part,
         send) = call(
            cross_backward,
            [((128, 768), F32), ((128, 768), BF), ((8, 768), F32), ((128, 384), BF),
             ((6, 128, 512), BF), ((6, 128, 512), BF), ((128, 384), BF)] + part_shape,
            xg, gains, ec, part, recv, resid_cross, *cw, cross_q, kva, kvb, cross_lse, mask,
            cross_mixed, hbm=(0, 2),
        )
        recv = row_swap(send)
        ci_keep, ci_send, co_keep, co_send, enc_keep, enc_send = call(
            cross_grads,
            [((1152, 384), BF), ((1152, 384), BF), ((192, 768), BF), ((192, 768), BF),
             ((2, 192, 512), F32), ((2, 192, 512), BF)],
            ec, normed_cross, cross_q, cross_delta, dscores, probs, cross_dq, cross_mixed,
            upstream_cross, *cw,)
        in_cross = core_sum(ci_keep, ci_send)
        out_cross = core_sum(co_keep, co_send)

        (grad_attn, gain_cross_sum, dscores, dya, dyb, si_keep, si_send, so_keep, so_send) = call(
            self_backward,
            [((128, 768), F32), ((8, 768), F32), ((6, 128, 256), F32), ((256, 576), BF),
             ((256, 576), BF), ((1152, 384), BF), ((1152, 384), BF), ((192, 768), BF),
             ((192, 768), BF)],
            xg, gains, part, recv, grad_cross, resid_attn, *sw, normed_self, ya, yb, bias,
            self_lse, self_mixed, hbm=(0, 1),
        )
        in_self = core_sum(si_keep, si_send)
        out_self = core_sum(so_keep, so_send)
        keep, send = call(self_inputs, part_shape, dya, dyb, *sw)
        keep, send = call(self_sum, part_shape, keep, col_swap(send))
        recv = row_swap(send)
        (tables,) = call(table_sums, [((2, 32, 128), F32)], buckets, dscores)
        grad_keep, grad_send, small_keep, small_send = call(
            last_norm,
            [((192, 128), F32), ((192, 128), F32), ((48, 128), F32), ((48, 128), F32)],
            xg, gains, keep, recv, grad_attn, gain_feed_sum, gain_cross_sum, tables,
        )

        def join(mine, theirs):
            return jnp.where(
                core == 0,
                jnp.concatenate((mine, theirs), axis=1),
                jnp.concatenate((theirs, mine), axis=1),
            ).T

        grad_hidden = join(grad_keep, col_swap(grad_send))

        out_keep, out_send = call(
            last_out, [((192, 128), BF), ((192, 128), BF)],
            last_keep, row_swap(last_send),
        )
        hidden_out = join(out_keep, col_swap(out_send))

        enc = enc_keep + col_swap(enc_send).astype(F32)
        grad_encoder = (enc[0] + row_swap(enc[1].astype(BF)).astype(F32)).T

        total = small_keep + col_swap(small_send)
        for bit in range(bits):
            total = total + replica_swap(total, bit)
        gain_grads = lax.dynamic_slice_in_dim(total[:9].reshape(3, 384), core * 192, 192, axis=1)
        table_grad = total[16:, :3]

        per = 384 // replicas
        wide = 512 // replicas
        short = 192 // replicas

        def blocks_of(values):
            return values.reshape(replicas, values.shape[0] // replicas, 768)

        feed_pair = scatter(in_feed.reshape(2, replicas, per, 1024), 1, forward)
        out_pair = scatter(blocks_of(out_feed), 0, backward)
        cross_pair = scatter(in_cross.reshape(3, replicas, per, 384), 1, forward)
        self_pair = scatter(in_self.reshape(3, replicas, per, 384), 1, forward)
        rest_pair = scatter(
            jnp.concatenate((blocks_of(out_cross), blocks_of(out_self)), axis=1), 0, forward
        )

        mine, send = call(
            finish_early, [((per, 1600), F32), ((per, 1600), BF)],
            *feed_pair, *cross_pair,
        )
        gate_grad, up_grad, keyvalue_grad, crossquery_grad = call(
            place_early,
            [((per, 1024), F32), ((per, 1024), F32), ((per, 768), F32), ((per, 384), F32)],
            mine, row_swap(send),
        )
        mine, send = call(
            finish_self, [((per, 576), F32), ((per, 576), BF)], *self_pair
        )
        querykey_grad, value_grad = call(
            place_self,
            [((per, 768), F32), ((per, 384), F32)],
            mine, row_swap(send),
        )

        sends = call(
            finish_out, [((wide + 2 * short, 384), BF)] * 2, *out_pair, *rest_pair
        )
        got = []
        for shift in (0, 1):
            moves = []
            for source in range(2 * replicas):
                replica, side = divmod(source, 2)
                block = side * replicas + replica
                moves.append((source, (block // 2) * 2 + ((block % 2) ^ shift)))
            got.append(lax.ppermute(sends[shift], ("dp", "row"), moves))
        down_grad, crossout_grad, output_grad = call(
            place_rows,
            [((2 * wide, 384), F32), ((2 * short, 384), F32), ((2 * short, 384), F32)], *got,
        )

        return (
            hidden_out, grad_hidden, grad_encoder, querykey_grad, value_grad, output_grad,
            crossquery_grad, keyvalue_grad, crossout_grad, gate_grad, up_grad, down_grad,
            gain_grads[0], gain_grads[1], gain_grads[2], table_grad,
        )

    return layer


def solution(mesh):
    tokens = P("dp", ("row", "col"))
    inward = P("row", "col")
    outward = P("col", "row")
    features = P(("row", "col"))
    inward_grad = P(("row", "dp"), "col")
    outward_grad = P(("col", "dp"), "row")
    bias = P(None, ("col", "row"))
    return jax.shard_map(
        build(mesh.shape["dp"]),
        mesh=mesh,
        in_specs=(
            tokens, tokens, P("dp", None), P("dp", None), P(), features, features, features,
            inward, inward, outward, inward, inward, outward, inward, inward, outward, bias,
            tokens,
        ),
        out_specs=(
            tokens, tokens, tokens, inward_grad, inward_grad, outward_grad, inward_grad,
            inward_grad, outward_grad, inward_grad, inward_grad, outward_grad, features, features,
            features, bias,
        ),
        check_vma=False,
    )
```

```python
import jax
import jax.numpy as jnp
from jax import lax
from jax.experimental import pallas as pl
from jax.experimental.pallas import tpu as pltpu
from jax.sharding import PartitionSpec as P


BF = jnp.bfloat16
F32 = jnp.float32
EPS = 1e-06
ROOT = 0.7978845608028654
CUBIC = 0.044715
MASKED = -1e30
SWAP = [(0, 1), (1, 0)]


def nn(left, right):
    return jnp.dot(left, right, preferred_element_type=F32)


def nt(left, right):
    return lax.dot_general(left, right, (((1,), (1,)), ((), ())), preferred_element_type=F32)


def tn(left, right):
    return lax.dot_general(left, right, (((0,), (0,)), ((), ())), preferred_element_type=F32)


def far(values):
    return pltpu.with_memory_space_constraint(values, pltpu.HBM)


def call(kernel, outs, *args, hbm=()):
    flat = [
        (pltpu.HBM if at in hbm else jax.ShapeDtypeStruct)(shape, dtype)
        for at, (shape, dtype) in enumerate(outs)
    ]
    space = pl.BlockSpec(memory_space=pltpu.VMEM)
    got = pl.pallas_call(
        kernel,
        out_shape=flat,
        in_specs=[space] * len(args),
        out_specs=[space] * len(flat),
        compiler_params=pltpu.CompilerParams(vmem_limit_bytes=16 * 1024 * 1024),
    )(*args)
    return [far(out) if at in hbm else out for at, out in enumerate(got)]


def row_swap(values):
    return lax.ppermute(values, "row", SWAP)


def col_swap(values):
    return lax.ppermute(values, "col", SWAP)


def own_rows(ref, base=0):
    half = 128
    start = base + lax.axis_index("col") * half
    return ref[pl.ds(pl.multiple_of(start, 16), half), :]


def each_side(axis, body):
    index = lax.axis_index(axis)
    for side in (0, 1):
        pl.when(index == side)(lambda side=side: body(side))


def swapped(ref, left, right):
    width = left.shape[1]
    ref[:, :width] = right.astype(BF)
    ref[:, width:] = left.astype(BF)


def each_replica(body):
    for part in range(4):
        pl.when(lax.axis_index("dp") % 4 == part)(lambda part=part: body(part))


def weight_parts(keep_body, send_body):
    def of_row(side):
        keep_body(side)
        each_replica(lambda part: send_body(1 - side, part))

    each_side("row", of_row)


def keep_cols(src, keep, at, width, side):
    keep[:, at : at + width] = src[:, side * width : (side + 1) * width]


def send_cols(src, send, at, width, side, part):
    rows = src.shape[0] // 4
    send[:, at : at + width] = src[
        part * rows : (part + 1) * rows, side * width : (side + 1) * width
    ]


def keep_out(src, keep, at, side):
    rows = src.shape[0] // 2
    width = src.shape[1] // 2
    for block in (0, 1):
        keep[block * rows : (block + 1) * rows, at : at + width] = src[
            side * rows : (side + 1) * rows, block * width : (block + 1) * width
        ]


def send_out(src, send, at, side, part):
    rows = src.shape[0] // 4
    width = src.shape[1] // 2
    start = side * 2 * rows + part % 2 * rows
    send[:, at : at + width] = src[
        start : start + rows, part // 2 * width : (part // 2 + 1) * width
    ]


def join_parts(parts, out):
    rows = parts[0].shape[0]
    place = lax.axis_index("dp") % 4
    for away, part in enumerate(parts):
        start = jnp.bitwise_xor(place, away) * rows
        out[pl.ds(pl.multiple_of(start, 16), rows), :] = part[...]


def assemble(own, recv, own_peer, recv_peer):
    core = lax.axis_index("col")
    first = core == 0
    quarters = (
        jnp.where(first, own[...], own_peer[...]),
        jnp.where(first, own_peer[...], own[...]),
        jnp.where(first, recv[...], recv_peer[...]),
        jnp.where(first, recv_peer[...], recv[...]),
    )
    return jnp.concatenate(quarters, axis=0)


def pack_three(wide, narrow, out, keep, send):
    def keep_body(side):
        keep_cols(wide, keep, 0, 384, side)
        keep_cols(narrow, keep, 384, 192, side)
        keep_out(out, keep, 576, side)

    def send_body(side, part):
        send_cols(wide, send, 0, 384, side, part)
        send_cols(narrow, send, 384, 192, side, part)
        send_out(out, send, 576, side, part)

    weight_parts(keep_body, send_body)


def prep_self(hidden, gs, gc, gf, qk, v, wo, packed, keep, send):
    tokens = hidden.shape[1]
    packed[:, :tokens] = hidden[...]
    gains = jnp.concatenate([gs[...], gc[...], gf[...]], axis=0)
    high = gains.astype(BF)
    low = (gains - high.astype(F32)).astype(BF)
    rows = jnp.concatenate(
        [high.astype(F32), low.astype(F32), jnp.zeros((10, gains.shape[1]), F32)], axis=0
    ).astype(BF)
    line = lax.broadcasted_iota(jnp.int32, (16, 16), 0)
    place = lax.broadcasted_iota(jnp.int32, (16, 16), 1)
    packed[:, tokens:] = tn(rows, jnp.where(line == place, 1.0, 0.0).astype(BF)).astype(BF)

    pack_three(qk, v, wo, keep, send)


def prep_cross(enc, cot, q, kv, wo, packed, keep, send):
    packed[:, : enc.shape[1]] = enc[...]
    packed[:, enc.shape[1] :] = cot[...]

    pack_three(kv, q, wo, keep, send)


def prep_feed(gate, up, down, keep, send, keep_down, send_down):
    def keep_body(side):
        keep_cols(gate, keep, 0, 512, side)
        keep_cols(up, keep, 512, 512, side)
        keep_down[...] = down[side * 512 : (side + 1) * 512, :]

    def send_body(side, part):
        send_cols(gate, send, 0, 512, side, part)
        send_cols(up, send, 512, 512, side, part)
        at = side * 512 + part * 128
        send_down[...] = down[at : at + 128, :]

    weight_parts(keep_body, send_body)


def masks(buckets, table, peer_table, segment, source, bias_out, cross_out):
    core = lax.axis_index("col")
    ids = own_rows(buckets)
    rows, cols = ids.shape
    line = lax.broadcasted_iota(jnp.int32, (rows, cols), 0) + core * rows
    place = lax.broadcasted_iota(jnp.int32, (rows, cols), 1)
    keys = segment[...]
    mine = jnp.sum(
        jnp.where(place == line, jnp.broadcast_to(keys, (rows, cols)).astype(F32), 0.0),
        axis=1,
        keepdims=True,
    )
    allowed = (place <= line) & (keys.astype(F32) == mine)
    for head in range(6):
        ref = table if head < 3 else peer_table
        entries = jnp.broadcast_to(ref[head % 3 : head % 3 + 1, :], (rows, 128))
        parts = [
            jnp.take_along_axis(
                entries, ids[:, at : at + 128], axis=1, mode="promise_in_bounds"
            )
            for at in range(0, cols, 128)
        ]
        bias_out[head] = jnp.where(allowed, jnp.concatenate(parts, axis=1), MASKED)
    cross_out[...] = jnp.where(source[...].astype(F32) == mine, 0.0, MASKED)


def gain_row(gains, which):
    return gains[which : which + 1, :]


def norm(resid, gain):
    scale = lax.rsqrt(jnp.mean(resid * resid, axis=1, keepdims=True) + EPS)
    return resid * scale * gain, scale


def norm_back(upstream, resid, gain):
    scale = lax.rsqrt(jnp.mean(resid * resid, axis=1, keepdims=True) + EPS)
    normed = resid * scale
    scaled = upstream * gain
    grad = scale * (scaled - normed * jnp.mean(scaled * normed, axis=1, keepdims=True))
    return grad, jnp.sum(upstream * normed, axis=0, keepdims=True)


def project(left, top, bottom, at, width):
    return nn(left[:, :384], top[:, at : at + width]) + nn(left[:, 384:], bottom[:, at : at + width])


def softmax(scores):
    top = jnp.max(scores, axis=1, keepdims=True)
    weights = jnp.exp(scores - top)
    total = jnp.sum(weights, axis=1, keepdims=True)
    return (weights * (1.0 / total)).astype(BF), top + jnp.log(total)


def out_project(mixed, a0, a1, b0, b1, keep, send):
    first, second = mixed[:, :192], mixed[:, 192:]
    parts = []
    for a, b in ((a0, b0), (a1, b1)):
        for block in (0, 1):
            lines = slice(block * 192, (block + 1) * 192)
            parts.append(nn(first, a[lines, 576:]) + nn(second, b[lines, 576:]))
    mine = jnp.concatenate(parts[:2], axis=1)
    theirs = jnp.concatenate(parts[2:], axis=1)
    keep[:, :384] = mine
    keep[:, 384:] = theirs
    swapped(send, mine, theirs)


def out_back(upstream, w0, w1):
    total = None
    for half, w in ((0, w0), (1, w1)):
        for block in (0, 1):
            at = half * 384 + block * 192
            term = nt(upstream[:, at : at + 192], w[block * 192 : (block + 1) * 192, 576:])
            total = term if total is None else total + term
    return total


def self_forward(
    own, recv, own_peer, recv_peer, a0, b0, p0, p1, p2, p3, q0, q1, q2, q3, bias, x_out, gains_out, a1, b1, normed_out, ya, yb, mixed_out, lse_out, keep, send,
):
    join_parts((p0, p1, p2, p3), a1)
    join_parts((q0, q1, q2, q3), b1)
    tokens = normed_out.shape[0]
    whole = assemble(own, recv, own_peer, recv_peer).astype(F32)
    resid = jnp.transpose(whole[:, :tokens])
    x_out[...] = resid.astype(BF)
    parts = whole[:, tokens:].astype(BF)
    line = lax.broadcasted_iota(jnp.int32, (16, 16), 0)
    place = lax.broadcasted_iota(jnp.int32, (16, 16), 1)
    chosen = (line == place) | ((line == place - 3) & (place < 6))
    chosen = jnp.where(chosen & (line < 3), 1.0, 0.0).astype(BF)
    gains_out[...] = nt(chosen, parts)
    normed = norm(resid, gain_row(gains_out, 0))[0].astype(BF)
    normed_out[...] = normed
    ya[...] = project(normed, a0, a1, 0, 576).astype(BF)
    yb[...] = project(normed, b0, b1, 0, 576).astype(BF)
    mixed = []
    for head in range(6):
        y = ya if head < 3 else yb
        at = (head % 3) * 128
        mine = own_rows(y)
        scores = nt(mine[:, at : at + 64], y[:, at + 64 : at + 128]) + bias[head]
        probs, lse = softmax(scores)
        lse_out[head] = lse
        at = 384 + (head % 3) * 64
        mixed.append(nn(probs, y[:, at : at + 64]))
    mixed = jnp.concatenate(mixed, axis=1).astype(BF)
    mixed_out[...] = mixed
    out_project(mixed, a0, a1, b0, b1, keep, send)


def encode_keys(
    own, recv, own_peer, recv_peer, a0, b0, p0, p1, p2, p3, q0, q1, q2, q3, ec, a1, b1, kva, kvb,
):
    join_parts((p0, p1, p2, p3), a1)
    join_parts((q0, q1, q2, q3), b1)
    rows = kva.shape[0]
    whole = assemble(own, recv, own_peer, recv_peer).astype(F32)
    ec[...] = jnp.transpose(whole).astype(BF)
    enc = ec[:rows, :]
    kva[...] = project(enc, a0, a1, 0, 384).astype(BF)
    kvb[...] = project(enc, b0, b1, 0, 384).astype(BF)


def cross_forward(
    xg, gains, part, recv, a0, a1, b0, b1, kva, kvb, mask, resid_out, normed_out, q_out, mixed_out,
    lse_out, keep, send,
):
    resid = own_rows(xg).astype(F32) + part[...] + recv[...].astype(F32)
    resid_out[...] = resid
    normed = norm(resid, gain_row(gains, 1))[0].astype(BF)
    normed_out[...] = normed
    queries = jnp.concatenate(
        [project(normed, a0, a1, 384, 192), project(normed, b0, b1, 384, 192)], axis=1
    ).astype(BF)
    q_out[...] = queries
    mixed = []
    for head in range(6):
        kv = kva if head < 3 else kvb
        at = (head % 3) * 128
        scores = nt(queries[:, head * 64 : head * 64 + 64], kv[:, at : at + 64]) + mask[...]
        probs, lse = softmax(scores)
        lse_out[head] = lse
        mixed.append(nn(probs, kv[:, at + 64 : at + 128]))
    mixed = jnp.concatenate(mixed, axis=1).astype(BF)
    mixed_out[...] = mixed
    out_project(mixed, a0, a1, b0, b1, keep, send)


def feed_upstream(ec, da0, db0, *refs):
    parts, (fa1, fb1, da1, db1, out) = refs[:16], refs[16:]
    for at, ref in enumerate((fa1, fb1, da1, db1)):
        join_parts(parts[at * 4 : at * 4 + 4], ref)
    cot = own_rows(ec, ec.shape[0] - 256)
    out[:, :512] = nt(cot[:, :384], da0[...]) + nt(cot[:, 384:], da1[...])
    out[:, 512:] = nt(cot[:, :384], db0[...]) + nt(cot[:, 384:], db1[...])


def feed_forward(
    xg, gains, prior, part, recv, fa0, fa1, fb0, fb1, upstream, resid_out, normed_out, hidden_out,
    gate_out, up_out, keep, send,
):
    resid = prior[...] + part[...] + recv[...].astype(F32)
    resid_out[...] = resid
    normed = norm(resid, gain_row(gains, 2))[0].astype(BF)
    normed_out[...] = normed
    deltas = []
    for side, (w0, w1) in enumerate(((fa0, fa1), (fb0, fb1))):
        lanes = slice(side * 512, side * 512 + 512)
        gate = project(normed, w0, w1, 0, 512)
        up = project(normed, w0, w1, 512, 512)
        inner = jnp.tanh(ROOT * (gate + CUBIC * gate * gate * gate))
        gelu = 0.5 * gate * (1.0 + inner)
        slope = 0.5 * (1.0 + inner) + 0.5 * gate * (1.0 - inner * inner) * ROOT * (
            1.0 + 3.0 * CUBIC * gate * gate
        )
        grad = upstream[:, lanes]
        hidden_out[:, lanes] = (gelu * up).astype(BF)
        gate_delta = (grad * up * slope).astype(BF)
        up_delta = (grad * gelu).astype(BF)
        gate_out[:, lanes] = gate_delta
        up_out[:, lanes] = up_delta
        deltas.append((gate_delta, up_delta))
    (ga, ua), (gb, ub) = deltas
    mine = nt(ga, fa0[:, :512]) + nt(ua, fa0[:, 512:]) + nt(gb, fb0[:, :512]) + nt(ub, fb0[:, 512:])
    theirs = (
        nt(ga, fa1[:, :512]) + nt(ua, fa1[:, 512:]) + nt(gb, fb1[:, :512]) + nt(ub, fb1[:, 512:])
    )
    keep[:, :384] = mine
    keep[:, 384:] = theirs
    swapped(send, mine, theirs)


def feed_grads(normed, gate, up, in_keep, in_send):
    left = normed[...]
    for ref, lanes in ((in_send, slice(512, 1024)), (in_keep, slice(0, 512))):
        ref[:, :512] = tn(left, gate[:, lanes]).astype(BF)
        ref[:, 512:] = tn(left, up[:, lanes]).astype(BF)


def feed_out(hidden, ec, resid, da0, da1, db0, db1, out_keep, out_send, last_keep, last_send):
    cot = own_rows(ec, ec.shape[0] - 256)
    out_send[...] = tn(hidden[:, 512:], cot).astype(BF)
    out_keep[...] = tn(hidden[:, :512], cot).astype(BF)
    last_send[...] = (nn(hidden[:, :512], da1[...]) + nn(hidden[:, 512:], db1[...])).astype(BF)
    last_keep[...] = (
        nn(hidden[:, :512], da0[...]) + nn(hidden[:, 512:], db0[...]) + resid[:, :384]
    )


def last_out(part, recv, keep, send):
    total = jnp.transpose(part[...] + recv[...].astype(F32)).astype(BF)

    def body(side):
        keep[...] = total[side * 192 : side * 192 + 192, :]
        send[...] = total[(1 - side) * 192 : (2 - side) * 192, :]

    each_side("col", body)


def store_grads(ref, left, wide, narrow, narrow_left):
    ref[:768, :] = tn(left, wide).astype(BF)
    thin = tn(narrow_left, narrow).astype(BF)
    ref[768:, :192] = thin[:384, :]
    ref[768:, 192:] = thin[384:, :]


def cross_backward(
    xg, gains, ec, part, recv, resid_in, a0, a1, b0, b1, q, kva, kvb, lse, mask, mixed, resid_out,
    upstream_out, gain_out, delta_out, dscores_out, probs_out, dq_out, keep, send,
):
    back, gain = norm_back(part[...] + recv[...].astype(F32), resid_in[...], gain_row(gains, 2))
    gain_out[...] = jnp.broadcast_to(gain, gain_out.shape)
    resid = own_rows(ec, ec.shape[0] - 256).astype(F32) + back
    resid_out[...] = resid
    upstream = resid.astype(BF)
    upstream_out[...] = upstream
    delta = jnp.concatenate(
        [out_back(upstream, a0, a1), out_back(upstream, b0, b1)], axis=1
    ).astype(BF)
    delta_out[...] = delta
    grads = []
    for head in range(6):
        kv = kva if head < 3 else kvb
        at = (head % 3) * 128
        lanes = slice(head * 64, head * 64 + 64)
        scores = nt(q[:, lanes], kv[:, at : at + 64]) + mask[...]
        probs = jnp.exp(scores - lse[head])
        probs_out[head] = probs.astype(BF)
        drift = nt(delta[:, lanes], kv[:, at + 64 : at + 128])
        centre = jnp.sum(
            delta[:, lanes].astype(F32) * mixed[:, lanes].astype(F32), axis=1, keepdims=True
        )
        low = (probs * (drift - centre)).astype(BF)
        dscores_out[head] = low
        grads.append(nn(low, kv[:, at : at + 64]))
    grads = jnp.concatenate(grads, axis=1).astype(BF)
    dq_out[...] = grads
    first, second = grads[:, :192], grads[:, 192:]
    mine = nt(first, a0[:, 384:576]) + nt(second, b0[:, 384:576])
    theirs = nt(first, a1[:, 384:576]) + nt(second, b1[:, 384:576])
    keep[:, :384] = mine
    keep[:, 384:] = theirs
    swapped(send, mine, theirs)


def cross_grads(
    ec, normed, q, delta, dscores, probs, dq, mixed, upstream, a0, a1, b0, b1, in_keep, in_send,
    out_keep, out_send, enc_keep, enc_send,
):
    rows = ec.shape[0] - 256
    enc = ec[:rows, :]
    left = normed[...]
    both = []
    for first in (0, 3):
        parts = []
        for head in range(first, first + 3):
            lanes = slice(head * 64, head * 64 + 64)
            parts.append(tn(dscores[head], q[:, lanes]))
            parts.append(tn(probs[head], delta[:, lanes]))
        both.append(jnp.concatenate(parts, axis=1).astype(BF))
    for ref, side in ((in_send, 1), (in_keep, 0)):
        store_grads(ref, enc, both[side], dq[:, side * 192 : side * 192 + 192], left)
    out_send[...] = tn(mixed[:, 192:], upstream[...]).astype(BF)
    out_keep[...] = tn(mixed[:, :192], upstream[...]).astype(BF)
    for half, (a, b) in enumerate(((a0, b0), (a1, b1))):
        total = nt(a[:, :384], both[0]) + nt(b[:, :384], both[1])

        def body(side, half=half, total=total):
            enc_keep[half] = total[side * 192 : side * 192 + 192, :]
            enc_send[half] = total[(1 - side) * 192 : (2 - side) * 192, :].astype(BF)

        each_side("col", body)


def self_backward(
    xg, gains, part, recv, upper, resid_in, a0, a1, b0, b1, normed, ya, yb, bias, lse, mixed, resid_out,
    gain_out, dscores_out, dya, dyb, in_keep, in_send, out_keep, out_send,
):
    back, gain = norm_back(part[...] + recv[...].astype(F32), resid_in[...], gain_row(gains, 1))
    gain_out[...] = jnp.broadcast_to(gain, gain_out.shape)
    resid = upper[...] + back
    resid_out[...] = resid
    upstream = resid.astype(BF)
    delta = jnp.concatenate(
        [out_back(upstream, a0, a1), out_back(upstream, b0, b1)], axis=1
    ).astype(BF)
    out_send[...] = tn(mixed[:, 192:], upstream).astype(BF)
    out_keep[...] = tn(mixed[:, :192], upstream).astype(BF)
    core = lax.axis_index("col").astype(F32)
    for y, dy, first in ((yb, dyb, 3), (ya, dya, 0)):
        mine = own_rows(y)
        pairs, values = [], []
        for head in range(first, first + 3):
            at = (head % 3) * 128
            vat = 384 + (head % 3) * 64
            lanes = slice(head * 64, head * 64 + 64)
            queries = mine[:, at : at + 64]
            scores = nt(queries, y[:, at + 64 : at + 128]) + bias[head]
            probs = jnp.exp(scores - lse[head])
            up = delta[:, lanes]
            drift = nt(up, y[:, vat : vat + 64])
            centre = jnp.sum(
                up.astype(F32) * mixed[:, lanes].astype(F32), axis=1, keepdims=True
            )
            dscores = probs * (drift - centre)
            dscores_out[head] = dscores
            low = dscores.astype(BF)
            dq = nn(low, y[:, at + 64 : at + 128])
            dq = jnp.concatenate([dq * (1.0 - core), dq * core], axis=0)
            pairs.append(jnp.concatenate([dq, tn(low, queries)], axis=1))
            values.append(tn(probs.astype(BF), up))
        dy[...] = jnp.concatenate(pairs + values, axis=1).astype(BF)
    left = normed[...]
    for ref, dy in ((in_send, dyb), (in_keep, dya)):
        store_grads(ref, left, dy[:, :384], dy[:, 384:], left)


def self_inputs(dya, dyb, a0, a1, b0, b1, keep, send):
    da, db = dya[...], dyb[...]
    totals = [nt(da, a[:, :576]) + nt(db, b[:, :576]) for a, b in ((a0, b0), (a1, b1))]

    def body(side):
        mine = slice(side * 128, side * 128 + 128)
        theirs = slice((1 - side) * 128, (1 - side) * 128 + 128)
        for at, total in ((0, totals[0]), (384, totals[1])):
            keep[:, at : at + 384] = total[mine, :]
            send[:, at : at + 384] = total[theirs, :].astype(BF)

    each_side("col", body)


def self_sum(part, other, keep, send):
    total = part[...] + other[...].astype(F32)
    keep[...] = total
    swapped(send, total[:, :384], total[:, 384:])


def table_sums(buckets, dscores, out):
    ids = own_rows(buckets)
    totals = []
    for head in range(6):
        grid = dscores[head]
        sums = []
        for label in range(32):
            chosen = jnp.where(ids == label, grid, 0.0)
            sums.append(jnp.sum(chosen, axis=0, keepdims=True))
        totals.append(jnp.sum(jnp.concatenate(sums, axis=0), axis=1, keepdims=True))
    place = lax.broadcasted_iota(jnp.int32, (32, 128), 1)
    for side in (0, 1):
        table = jnp.zeros((32, 128), F32)
        for head in range(3):
            table = jnp.where(place == head, totals[side * 3 + head], table)
        out[side] = table


def last_norm(
    xg, gains, part, recv, upper, gain_feed, gain_cross, tables, keep, send, small_keep,
    small_send,
):
    resid = own_rows(xg).astype(F32)
    back, gain = norm_back(part[...] + recv[...].astype(F32), resid, gain_row(gains, 0))
    total = jnp.transpose((upper[...] + back)[:, :384])

    def body(side):
        keep[...] = total[side * 192 : side * 192 + 192, :]
        send[...] = total[(1 - side) * 192 : (2 - side) * 192, :]

    each_side("col", body)
    rows = []
    for values in (gain, gain_cross[:1, :], gain_feed[:1, :]):
        rows += [values[:, at : at + 128] for at in (0, 128, 256)]
    rows = jnp.concatenate(rows + [jnp.zeros((7, 128), F32)], axis=0)
    small_keep[:16, :] = rows
    small_send[:16, :] = rows
    small_keep[16:, :] = tables[0]
    small_send[16:, :] = tables[1]


def split_blocks(blocks, count, at, bit, mine, send):
    per = mine.shape[0] * 2 // count

    def body(value):
        for block in range(count):
            place = ((block >> (at + 1)) << at) | (block & ((1 << at) - 1))
            ref = mine if ((block >> at) & 1) == value else send
            ref[place * per : (place + 1) * per, :] = blocks(block)

    for value in (0, 1):
        pl.when(((lax.axis_index("dp") >> bit) & 1) == value)(lambda value=value: body(value))


def stage_of(count, at, bit):
    def halve_blocks(keep, recv, mine, send):
        per = keep.shape[0] // count

        def total(block):
            lines = slice(block * per, (block + 1) * per)
            return (keep[lines, :].astype(F32) + recv[lines, :].astype(F32)).astype(BF)

        split_blocks(total, count, at, bit, mine, send)

    return halve_blocks


def halve_pair(count, bit):
    def halve_outs(keep, recv, other_keep, other_recv, mine, send):
        per = keep.shape[0] // count

        def total(block):
            lines = slice(block * per, (block + 1) * per)
            first = keep[lines, :].astype(F32) + recv[lines, :].astype(F32)
            second = other_keep[lines, :].astype(F32) + other_recv[lines, :].astype(F32)
            return jnp.concatenate([first, second], axis=0).astype(BF)

        split_blocks(total, count, 0, bit, mine, send)

    return halve_outs


def finish_early(feed_keep, feed_recv, cross_keep, cross_recv, mine, send):
    for half, ref in ((0, mine), (1, send)):
        feed = feed_keep[half].astype(F32) + feed_recv[half].astype(F32)
        wide = cross_keep[half].astype(F32) + cross_recv[half].astype(F32)
        thin = cross_keep[2].astype(F32) + cross_recv[2].astype(F32)
        ref[:, :1024] = feed.astype(ref.dtype)
        ref[:, 1024:1408] = wide.astype(ref.dtype)
        ref[:, 1408:] = thin[:, half * 192 : half * 192 + 192].astype(ref.dtype)


def finish_self(keep, recv, mine, send):
    for half, ref in ((0, mine), (1, send)):
        wide = keep[half].astype(F32) + recv[half].astype(F32)
        thin = keep[2].astype(F32) + recv[2].astype(F32)
        ref[:, :384] = wide.astype(ref.dtype)
        ref[:, 384:] = thin[:, half * 192 : half * 192 + 192].astype(ref.dtype)


def place_columns(widths, mine, recv, *outs):
    def body(side):
        at = 0
        for width, out in zip(widths, outs):
            first = mine[:, at : at + width]
            second = recv[:, at : at + width].astype(F32)
            if side:
                first, second = second, first
            out[:, :width] = first
            out[:, width:] = second
            at += width

    each_side("row", body)


def place_early(mine, recv, *outs):
    place_columns((512, 512, 384, 192), mine, recv, *outs)


def place_self(mine, recv, *outs):
    place_columns((384, 192), mine, recv, *outs)


def finish_out(feed_keep, feed_recv, rest_keep, rest_recv, first, second):
    total = jnp.concatenate(
        [
            feed_keep[...].astype(F32) + feed_recv[...].astype(F32),
            rest_keep[...].astype(F32) + rest_recv[...].astype(F32),
        ],
        axis=0,
    ).astype(BF)
    swap = (lax.axis_index("dp") + lax.axis_index("row")) % 2

    def body(side):
        for ref, half in ((first, side), (second, 1 - side)):
            ref[...] = total[:, half * 384 : half * 384 + 384]

    for side in (0, 1):
        pl.when(swap == side)(lambda side=side: body(side))


def place_rows(first, second, *outs):
    def body(side):
        at = 0
        for out in outs:
            size = out.shape[0] // 2
            parts = [ref[at : at + size, :].astype(F32) for ref in (first, second)]
            if side:
                parts = parts[::-1]
            out[:size, :] = parts[0]
            out[size:, :] = parts[1]
            at += size

    each_side("row", body)


def build(replicas):
    bits = replicas.bit_length() - 1
    assert 1 << bits == replicas and replicas % 2 == 0

    def replica_swap(values, bit):
        return lax.ppermute(values, "dp", [(i, i ^ (1 << bit)) for i in range(replicas)])

    def scatter(values, axis, order):
        place = lax.axis_index("dp")
        shape = values.shape
        values = values.reshape(shape[:axis] + (2,) * bits + shape[axis + 1 :])
        left = list(range(bits - 1, -1, -1))
        for bit in order:
            at = axis + left.index(bit)
            left.remove(bit)
            mine = (place >> bit) & 1
            keep = lax.dynamic_index_in_dim(values, mine, at, keepdims=False)
            send = lax.dynamic_index_in_dim(values, 1 - mine, at, keepdims=False)
            recv = replica_swap(send, bit)
            values = (keep.astype(F32) + recv.astype(F32)).astype(BF)
        return keep, recv

    def halvings(keep, recv, groups, order):
        per = keep.shape[0] // (groups * replicas)
        left = list(range(bits - 1, -1, -1))
        for bit in order:
            at = len(left) - 1 - left.index(bit)
            count = groups << len(left)
            shape = ((keep.shape[0] // 2, keep.shape[1]), BF)
            keep, send = call(stage_of(count, at, bit), [shape, shape], keep, recv)
            left.remove(bit)
            recv = replica_swap(send, bit)
        shape = (groups, per, keep.shape[1]) if groups > 1 else (per, keep.shape[1])
        return keep.reshape(shape), recv.reshape(shape)

    def spread(values):
        direct = row_swap(values)
        beside = replica_swap(direct, 0)
        parts = (direct, beside, replica_swap(direct, 1), replica_swap(beside, 1))
        return parts, tuple(col_swap(part) for part in parts)

    def add(keep, recv):
        return (keep.astype(F32) + recv.astype(F32)).astype(BF)

    def layer(
        hidden_in, encoder_states, token_segments, source_segments, buckets, gain_self, gain_cross,
        gain_feed, self_querykey, self_value, self_output, cross_query, cross_keyvalue,
        cross_output, gate_weight, up_weight, down_weight, bias_table, cotangent,
    ):
        core = lax.axis_index("col")
        (buckets, self_querykey, self_value, self_output, cross_query, cross_keyvalue,
         cross_output, gate_weight, up_weight, down_weight, token_segments, source_segments) = map(
            far,
            (buckets, self_querykey, self_value, self_output, cross_query, cross_keyvalue,
             cross_output, gate_weight, up_weight, down_weight, token_segments, source_segments),
        )
        forward = list(range(bits))
        backward = list(range(1, bits)) + [0]

        packed, s_keep, s_send = call(
            prep_self,
            [((192, 272), BF), ((384, 768), BF), ((96, 768), BF)],
            far(hidden_in.T), far(gain_self[None]), far(gain_cross[None]), far(gain_feed[None]), self_querykey,
            self_value, self_output,
        )
        x_row = row_swap(packed)
        s_parts, s_peers = spread(s_send)
        s_other = col_swap(s_keep)
        table = jnp.pad(bias_table.T, ((0, 5), (0, 96)))
        peer_table = col_swap(table)
        bias, mask = call(
            masks, [((6, 128, 256), F32), ((128, 512), F32)],
            buckets, table, peer_table, token_segments, source_segments, hbm=(0, 1),
        )

        e_pack, c_keep, c_send = call(
            prep_cross,
            [((192, 768), BF), ((384, 768), BF), ((96, 768), BF)],
            far(encoder_states.T), far(cotangent.T), cross_query, cross_keyvalue, cross_output,
        )
        e_row = row_swap(e_pack)
        c_parts, c_peers = spread(c_send)
        c_other = col_swap(c_keep)

        f_keep, f_send, d_keep, d_send = call(
            prep_feed,
            [((384, 1024), BF), ((96, 1024), BF), ((512, 384), BF), ((128, 384), BF)],
            gate_weight, up_weight, down_weight,
        )
        d_parts, d_peers = spread(d_send)
        f_parts, f_peers = spread(f_send)
        f_other = col_swap(f_keep)
        d_other = col_swap(d_keep)

        part_shape = [((128, 768), F32), ((128, 768), BF)]
        matrix = [((384, 768), BF), ((384, 768), BF)]
        xg, gains, s_a1, s_b1, normed_self, ya, yb, self_mixed, self_lse, part, send = call(
            self_forward,
            [((256, 768), BF), ((16, 768), F32)] + matrix + [((256, 768), BF), ((256, 576), BF),
             ((256, 576), BF), ((128, 384), BF), ((6, 128, 1), F32)] + part_shape,
            packed, x_row, col_swap(packed), col_swap(x_row), s_keep, s_other,
            *s_parts, *s_peers, bias, hbm=(0, 1, 2, 3, 4, 5, 6, 7, 8),
        )
        sw = (far(s_keep), s_a1, far(s_other), s_b1)
        recv = row_swap(send)
        ec, c_a1, c_b1, kva, kvb = call(
            encode_keys,
            [((768, 768), BF)] + matrix + [((512, 384), BF), ((512, 384), BF)],
            e_pack, e_row, col_swap(e_pack), col_swap(e_row), c_keep, c_other,
            *c_parts, *c_peers, hbm=(0, 1, 2, 3, 4),
        )
        cw = (far(c_keep), c_a1, far(c_other), c_b1)
        resid_attn, normed_cross, cross_q, cross_mixed, cross_lse, part, send = call(
            cross_forward,
            [((128, 768), F32), ((128, 768), BF), ((128, 384), BF), ((128, 384), BF),
             ((6, 128, 1), F32)] + part_shape,
            xg, gains, part, recv, *cw, kva, kvb, mask, hbm=(0, 1, 2, 3, 4),
        )
        recv = row_swap(send)
        f_a1, f_b1, d_a1, d_b1, upstream = call(
            feed_upstream,
            [((384, 1024), BF), ((384, 1024), BF), ((512, 384), BF), ((512, 384), BF),
             ((128, 1024), F32)],
            ec, d_keep, d_other, *f_parts, *f_peers, *d_parts, *d_peers, hbm=(2, 3),
        )
        dw = (far(d_keep), d_a1, far(d_other), d_b1)
        resid_cross, normed_feed, hidden, gate_delta, up_delta, part, send = call(
            feed_forward,
            [((128, 768), F32), ((128, 768), BF), ((128, 1024), BF), ((128, 1024), BF),
             ((128, 1024), BF)] + part_shape,
            xg, gains, resid_attn, part, recv, f_keep, f_a1, f_other, f_b1, upstream, hbm=(0, 2),
        )
        recv = row_swap(send)
        fi_keep, fi_send = call(
            feed_grads, [((768, 1024), BF), ((768, 1024), BF)],
            normed_feed, gate_delta, up_delta,)
        fi_recv = col_swap(fi_send)
        fo_keep, fo_send, last_keep, last_send = call(
            feed_out,
            [((512, 768), BF), ((512, 768), BF), ((128, 384), F32), ((128, 384), BF)],
            hidden, ec, resid_cross, *dw, hbm=(2,),
        )
        fo_recv = col_swap(fo_send)

        (grad_cross, upstream_cross, gain_feed_sum, cross_delta, dscores, probs, cross_dq, part,
         send) = call(
            cross_backward,
            [((128, 768), F32), ((128, 768), BF), ((8, 768), F32), ((128, 384), BF),
             ((6, 128, 512), BF), ((6, 128, 512), BF), ((128, 384), BF)] + part_shape,
            xg, gains, ec, part, recv, resid_cross, *cw, cross_q, kva, kvb, cross_lse, mask,
            cross_mixed, hbm=(0, 2),
        )
        recv = row_swap(send)
        ci_keep, ci_send, co_keep, co_send, enc_keep, enc_send = call(
            cross_grads,
            [((1152, 384), BF), ((1152, 384), BF), ((192, 768), BF), ((192, 768), BF),
             ((2, 192, 512), F32), ((2, 192, 512), BF)],
            ec, normed_cross, cross_q, cross_delta, dscores, probs, cross_dq, cross_mixed,
            upstream_cross, *cw,)
        ci_recv = col_swap(ci_send)
        co_recv = col_swap(co_send)

        (grad_attn, gain_cross_sum, dscores, dya, dyb, si_keep, si_send, so_keep, so_send) = call(
            self_backward,
            [((128, 768), F32), ((8, 768), F32), ((6, 128, 256), F32), ((256, 576), BF),
             ((256, 576), BF), ((1152, 384), BF), ((1152, 384), BF), ((192, 768), BF),
             ((192, 768), BF)],
            xg, gains, part, recv, grad_cross, resid_attn, *sw, normed_self, ya, yb, bias,
            self_lse, self_mixed, hbm=(0, 1),
        )
        si_recv = col_swap(si_send)
        so_recv = col_swap(so_send)
        keep, send = call(self_inputs, part_shape, dya, dyb, *sw)
        keep, send = call(self_sum, part_shape, keep, col_swap(send))
        recv = row_swap(send)
        (tables,) = call(table_sums, [((2, 32, 128), F32)], buckets, dscores)
        grad_keep, grad_send, small_keep, small_send = call(
            last_norm,
            [((192, 128), F32), ((192, 128), F32), ((48, 128), F32), ((48, 128), F32)],
            xg, gains, keep, recv, grad_attn, gain_feed_sum, gain_cross_sum, tables,
        )

        def join(mine, theirs):
            return jnp.where(
                core == 0,
                jnp.concatenate((mine, theirs), axis=1),
                jnp.concatenate((theirs, mine), axis=1),
            ).T

        grad_hidden = join(grad_keep, col_swap(grad_send))

        out_keep, out_send = call(
            last_out, [((192, 128), BF), ((192, 128), BF)],
            last_keep, row_swap(last_send),
        )
        hidden_out = join(out_keep, col_swap(out_send))

        enc = enc_keep + col_swap(enc_send).astype(F32)
        grad_encoder = (enc[0] + row_swap(enc[1].astype(BF)).astype(F32)).T

        total = small_keep + col_swap(small_send)
        for bit in range(bits):
            total = total + replica_swap(total, bit)
        gain_grads = lax.dynamic_slice_in_dim(total[:9].reshape(3, 384), core * 192, 192, axis=1)
        table_grad = total[16:, :3]

        per = 384 // replicas
        wide = 512 // replicas
        short = 192 // replicas

        def blocks_of(values):
            return values.reshape(replicas, values.shape[0] // replicas, 768)

        if per % 16 == 0:
            feed_pair = halvings(fi_keep, fi_recv, 2, forward)
            out_pair = halvings(fo_keep, fo_recv, 1, backward)
            cross_pair = halvings(ci_keep, ci_recv, 3, forward)
            self_pair = halvings(si_keep, si_recv, 3, forward)
            shape = ((192, 768), BF)
            keep, send = call(
                halve_pair(replicas, 0), [shape, shape], co_keep, co_recv, so_keep, so_recv
            )
            recv = replica_swap(send, 0)
            for bit in forward[1:]:
                shape = ((keep.shape[0] // 2, 768), BF)
                keep, send = call(
                    stage_of(replicas >> bit, 0, bit), [shape, shape], keep, recv
                )
                recv = replica_swap(send, bit)
            rest_pair = (keep, recv)
        else:
            in_feed, out_feed = add(fi_keep, fi_recv), add(fo_keep, fo_recv)
            in_cross, in_self = add(ci_keep, ci_recv), add(si_keep, si_recv)
            out_cross, out_self = add(co_keep, co_recv), add(so_keep, so_recv)
            feed_pair = scatter(in_feed.reshape(2, replicas, per, 1024), 1, forward)
            out_pair = scatter(blocks_of(out_feed), 0, backward)
            cross_pair = scatter(in_cross.reshape(3, replicas, per, 384), 1, forward)
            self_pair = scatter(in_self.reshape(3, replicas, per, 384), 1, forward)
            rest_pair = scatter(
                jnp.concatenate((blocks_of(out_cross), blocks_of(out_self)), axis=1), 0, forward,
            )

        mine, send = call(
            finish_early, [((per, 1600), F32), ((per, 1600), BF)],
            *feed_pair, *cross_pair,
        )
        gate_grad, up_grad, keyvalue_grad, crossquery_grad = call(
            place_early,
            [((per, 1024), F32), ((per, 1024), F32), ((per, 768), F32), ((per, 384), F32)],
            mine, row_swap(send),
        )
        mine, send = call(
            finish_self, [((per, 576), F32), ((per, 576), BF)], *self_pair
        )
        querykey_grad, value_grad = call(
            place_self,
            [((per, 768), F32), ((per, 384), F32)],
            mine, row_swap(send),
        )

        sends = call(
            finish_out, [((wide + 2 * short, 384), BF)] * 2, *out_pair, *rest_pair
        )
        got = []
        for shift in (0, 1):
            moves = []
            for source in range(2 * replicas):
                replica, side = divmod(source, 2)
                block = side * replicas + replica
                moves.append((source, (block // 2) * 2 + ((block % 2) ^ shift)))
            got.append(lax.ppermute(sends[shift], ("dp", "row"), moves))
        down_grad, crossout_grad, output_grad = call(
            place_rows,
            [((2 * wide, 384), F32), ((2 * short, 384), F32), ((2 * short, 384), F32)], *got,
        )

        return (
            hidden_out, grad_hidden, grad_encoder, querykey_grad, value_grad, output_grad,
            crossquery_grad, keyvalue_grad, crossout_grad, gate_grad, up_grad, down_grad,
            gain_grads[0], gain_grads[1], gain_grads[2], table_grad,
        )

    return layer


def solution(mesh):
    tokens = P("dp", ("row", "col"))
    inward = P("row", "col")
    outward = P("col", "row")
    features = P(("row", "col"))
    inward_grad = P(("row", "dp"), "col")
    outward_grad = P(("col", "dp"), "row")
    bias = P(None, ("col", "row"))
    return jax.shard_map(
        build(mesh.shape["dp"]),
        mesh=mesh,
        in_specs=(
            tokens, tokens, P("dp", None), P("dp", None), P(), features, features, features,
            inward, inward, outward, inward, inward, outward, inward, inward, outward, bias,
            tokens,
        ),
        out_specs=(
            tokens, tokens, tokens, inward_grad, inward_grad, outward_grad, inward_grad,
            inward_grad, outward_grad, inward_grad, inward_grad, outward_grad, features, features,
            features, bias,
        ),
        check_vma=False,
    )
```
